256 devices in a mesh: expert: 32 (over x, y, core), dp: 8 (over z).
Axes of the slice: x: 4, y: 4, z: 8, core: 2. Of those that a mesh axis runs over, the one named last changes fastest.
Arguments:
- tokens: bfloat16 [32768, 1024], P(('expert', 'dp')), may hold values from -6 to 6
- expert_ids: int32 [32768, 8], P(('expert', 'dp')), may hold values from 0 to 63, all different within a row; in each aligned block of 128 rows (0 to 127, 128 to 255, ...) at most 24 rows name the same one
- combine_weights: float32 [32768, 8], P(('expert', 'dp')), may hold values from 0.2 to 1
- lift_weights: bfloat16 [64, 1024, 768], P('expert', 'dp'), may hold values from -0.1875 to 0.1875
- down_weights: bfloat16 [64, 384, 1024], P('expert', None, 'dp'), may hold values from -0.3125 to 0.3125
- cotangent: bfloat16 [32768, 1024], P(('expert', 'dp')), may hold values from -1.5 to 1.5
Outputs:
- layer_output: bfloat16 [32768, 1024], P(('expert', 'dp'))
- token_grads: bfloat16 [32768, 1024], P(('expert', 'dp'))
- lift_grads: bfloat16 [64, 1024, 768], P('expert', 'dp')
- down_grads: bfloat16 [64, 384, 1024], P('expert', None, 'dp')
The draws below stay inside these ranges and needn't reach their ends.
Inputs may be any that keep to these rules, and one draw needn't show every extreme that they name: `expert_ids`: each row names 8 different experts. Among the 128 rows of one device, no expert is named more than 24 times, and in every draw some expert is named exactly 24 times in some device's rows.
All inputs are finite; a program needn't handle non-finite values.
Results may differ from the reference program's by a relative error of at most 0.02.
Values may be sent and summed in bfloat16 or wider, within the bound.
No kernel may reach another device: no remote copies, remote signals or barrier semaphores. Data moves between devices by JAX's collectives and lax.ppermute only.
A program may use at most 64 MiB of HBM per device.

```python
import math
import jax
import jax.numpy as jnp
import numpy as np
from jax import lax

D = 1024
FF = 384
TOPK = 8
TOK_DEV = 128
EXPERTS = 64
TOKENS = 32768
CAP = 24
N_EXPERT = 32
N_DP = 8


def block_scale(rng, dims, pieces, least, high):
    gain = 1.0
    for dim, blocks in pieces:
        heights = jax.random.uniform(jax.random.fold_in(jax.random.fold_in(rng, 6), dim), (blocks,), jnp.float32, least / len(pieces), high / len(pieces))
        gain = gain * jnp.repeat(jnp.exp(heights), dims[dim] // blocks).reshape((-1,) + (1,) * (len(dims) - 1 - dim))
    return gain


def assign_block(rng, own, number, rows, count, top, most, skew):
    order = jax.random.permutation(rng, count)
    packed, common = shares(count, rows * top, most, skew, True), shares(count, rows * top, most, skew, False)
    places = jnp.arange(count)

    def named(sizes, turn):
        used = int((sizes > 0).sum())
        fixed = max(1, used // 4)
        passed = fixed + (places - fixed + turn * (used - fixed)) % max(1, count - fixed)
        return jnp.zeros((count,), jnp.int32).at[order[jnp.where(places < fixed, places, passed)]].set(jnp.asarray(sizes, jnp.int32))

    sizes = jnp.where(number % 4 == 0, named(packed, number // 4), named(common, number - number // 4 - 1))
    mixed = jax.random.permutation(jax.random.fold_in(own, 3), count)
    donor, sink = mixed[0:count // 2 * 2:2], mixed[1:count // 2 * 2:2]
    margin = jnp.minimum(sizes[donor] - 1, most - sizes[sink]) // 2
    margin = jnp.where((donor == order[0]) | (sink == order[0]) | (sizes[sink] == 0), 0, jnp.maximum(margin, 0))
    passed = jax.random.randint(jax.random.fold_in(own, 4), (count // 2,), 0, 1 << 20) % (margin + 1)
    sizes = sizes.at[donor].add(-passed).at[sink].add(passed)
    members = jnp.searchsorted(jnp.cumsum(sizes), jnp.arange(rows * top), side="right").astype(jnp.int32)
    listing = members.reshape(top, rows).T
    listing = listing[jax.random.permutation(jax.random.fold_in(own, 1), rows)]
    turn = jax.random.randint(jax.random.fold_in(own, 2), (rows, 1), 0, top)
    return jnp.take_along_axis(listing, (jnp.arange(top)[None, :] + turn) % top, axis=1)


def shares(number_of, total, limit, slope, full):
    weights = [(1 << 20) // math.isqrt(rank ** slope) + 1 for rank in range(1, number_of + 1)]
    largest = limit if full else min(limit, max(-(-total // number_of), total * weights[0] // sum(weights)))
    least = 1 if total - largest >= number_of - 1 else 0
    holding, spare = [largest] + [least] * (number_of - 1), total - largest - least * (number_of - 1)
    while spare > 0:
        movable = [i for i in range(1, number_of) if holding[i] < largest] or [i for i in range(1, number_of) if holding[i] < limit]
        whole, remaining = sum([weights[i] for i in movable]), spare
        for i in movable:
            addition = min(limit - holding[i], max(1, remaining * weights[i] // whole), spare)
            holding[i] = holding[i] + addition
            spare = spare - addition
    return np.array(holding)


def scatter_about(rng, shape, spread, bound, split=(), kind=jnp.bfloat16):
    entries = jax.random.normal(rng, shape, jnp.float32) * spread
    if len(split) > 0:
        entries = block_scale(rng, shape, split, -0.22, 0.18) * entries
    return jnp.clip(entries, min=-bound, max=bound).astype(kind)


def setup_inputs(seed: int = 0) -> dict:
    key_list = jax.random.split(jax.random.key(seed), 7)
    tokens = scatter_about(key_list[0], (TOKENS, D), 1.0, 6.0, ((0, 256),))
    expert_ids_keys = jax.random.split(jax.random.fold_in(key_list[1], 1), TOKENS // TOK_DEV)
    expert_ids_turns = jax.random.permutation(jax.random.fold_in(key_list[1], 3), TOKENS // TOK_DEV)
    expert_ids = jax.vmap(lambda own, number: assign_block(jax.random.fold_in(key_list[1], 2), own, number, TOK_DEV, EXPERTS, TOPK, CAP, 2))(expert_ids_keys, expert_ids_turns).reshape((TOKENS, TOPK))
    combine_weights = jnp.clip(0.2 + 0.8 * jax.random.uniform(key_list[2], (TOKENS, TOPK), jnp.float32) ** block_scale(key_list[2], (TOKENS, TOPK), ((0, 256),), -0.2, 0.2), 0.2, 1.0)
    lift_weights = scatter_about(key_list[3], (EXPERTS, D, 2 * FF), D ** -0.5, 0.1875, ((0, 32), (1, 8)))
    down_weights = scatter_about(key_list[4], (EXPERTS, FF, D), FF ** -0.5, 0.3125, ((0, 32), (2, 8)))
    cotangent = scatter_about(key_list[5], (TOKENS, D), 0.25, 1.5, ((0, 256),))
    return {"tokens": tokens, "expert_ids": expert_ids, "combine_weights": combine_weights, "lift_weights": lift_weights, "down_weights": down_weights, "cotangent": cotangent}


def swish_parts(gate_part):
    sigmoid_val = jax.nn.sigmoid(gate_part)
    return gate_part * sigmoid_val, sigmoid_val * (1.0 + gate_part * (1.0 - sigmoid_val))


def rounded_sum(total, term):
    narrow = lax.optimization_barrier(term.astype(jnp.bfloat16))
    return total + narrow.astype(jnp.float32)


def reference(tokens, expert_ids, combine_weights, lift_weights, down_weights, cotangent):
    capacity_rows = N_EXPERT * CAP
    token_group = (jnp.arange(TOKENS, dtype=jnp.int32) // TOK_DEV) % N_DP
    group_keys = (expert_ids * N_DP + token_group[:, None]).reshape(-1).astype(jnp.int32)
    ordering = jnp.argsort(group_keys, stable=True).astype(jnp.int32)
    counted = jnp.zeros((EXPERTS * N_DP,), jnp.int32).at[group_keys].add(1)
    starting = (jnp.cumsum(counted) - counted).astype(jnp.int32)
    ordering = jnp.concatenate([ordering, jnp.zeros((capacity_rows,), jnp.int32)])
    flat_weights = combine_weights.reshape(-1)
    positions = jnp.arange(capacity_rows, dtype=jnp.int32)

    def per_expert(running, expert):
        out_sum, grad_sum = running
        lift_matrix = lift_weights[expert]
        down_matrix = down_weights[expert]
        lift_total = jnp.zeros((D, 2 * FF), jnp.float32)
        down_total = jnp.zeros((FF, D), jnp.float32)
        for group_index in range(N_DP):
            pair_key = expert * N_DP + group_index
            picked = lax.dynamic_slice(ordering, (starting[pair_key],), (capacity_rows,))
            is_valid = positions < counted[pair_key]
            row_ids = picked // TOPK
            weight_vals = jnp.where(is_valid, flat_weights[picked], jnp.zeros((), flat_weights.dtype))
            inputs = jnp.where(is_valid[:, None], tokens[row_ids], jnp.zeros((), tokens.dtype))
            back_in = (weight_vals[:, None] * cotangent[row_ids].astype(jnp.float32)).astype(jnp.bfloat16)
            hidden = jnp.dot(inputs, lift_matrix, preferred_element_type=jnp.float32)
            gate_part = hidden[:, :FF]
            up_part = hidden[:, FF:]
            swished, slopes = swish_parts(gate_part)
            activated = (swished * up_part).astype(jnp.bfloat16)
            result = jnp.dot(activated, down_matrix, preferred_element_type=jnp.float32).astype(jnp.bfloat16)
            out_sum = out_sum.at[row_ids].add(weight_vals[:, None] * result.astype(jnp.float32))
            grad_act = jnp.dot(back_in, down_matrix.T, preferred_element_type=jnp.float32)
            grad_hidden = jnp.concatenate([grad_act * up_part * slopes, grad_act * swished], axis=1).astype(jnp.bfloat16)
            grad_rows = jnp.dot(grad_hidden, lift_matrix.T, preferred_element_type=jnp.float32).astype(jnp.bfloat16)
            grad_sum = grad_sum.at[row_ids].add(jnp.where(is_valid[:, None], grad_rows.astype(jnp.float32), jnp.zeros((), jnp.float32)))
            lift_total = rounded_sum(lift_total, jnp.dot(inputs.T, grad_hidden, preferred_element_type=jnp.float32))
            down_total = rounded_sum(down_total, jnp.dot(activated.T, back_in, preferred_element_type=jnp.float32))
        return (out_sum, grad_sum), (lift_total.astype(jnp.bfloat16), down_total.astype(jnp.bfloat16))

    start_sums = (jnp.zeros((TOKENS, D), jnp.float32), jnp.zeros((TOKENS, D), jnp.float32))
    sums_out, grads_out = lax.scan(per_expert, start_sums, jnp.arange(EXPERTS, dtype=jnp.int32))
    out_sum, grad_sum = sums_out
    lift_grads, down_grads = grads_out
    return out_sum.astype(jnp.bfloat16), grad_sum.astype(jnp.bfloat16), lift_grads, down_grads
```

```python
import functools
import jax
import jax.numpy as jnp
from jax import lax
from jax.experimental import pallas as pl
from jax.experimental.pallas import tpu as pltpu
from jax.sharding import PartitionSpec as P

BF = jnp.bfloat16
F32 = jnp.float32
CAP = 24
VMEM_LIMIT = 56 << 20


def call(kernel, name, out_shape, grid=None, in_specs=None, out_specs=None, scratch=(), flops=0, nbytes=0):
    full = pl.BlockSpec(memory_space=pltpu.VMEM)
    kwargs = {} if grid is None else {"grid": grid}
    return pl.pallas_call(
        kernel,
        name=name,
        out_shape=out_shape,
        in_specs=in_specs,
        out_specs=full if out_specs is None else out_specs,
        scratch_shapes=scratch,
        compiler_params=pltpu.CompilerParams(vmem_limit_bytes=VMEM_LIMIT),
        cost_estimate=pl.CostEstimate(flops=flops, transcendentals=0, bytes_accessed=nbytes),
        **kwargs,
    )


def membership(ids, weights, experts):
    rows, top = ids.shape
    lane = lax.broadcasted_iota(jnp.int32, (rows, experts), 1)
    named = jnp.zeros((rows, experts), F32)
    gates = jnp.zeros((rows, experts), F32)
    for k in range(top):
        hit = ids[:, k : k + 1] == lane
        named = jnp.where(hit, 1.0, named)
        if weights is not None:
            gates = jnp.where(hit, weights[:, k : k + 1], gates)
    before = (
        lax.broadcasted_iota(jnp.int32, (rows, rows), 1)
        < lax.broadcasted_iota(jnp.int32, (rows, rows), 0)
    ).astype(F32).astype(BF)
    rank = jnp.dot(before, named.astype(BF), preferred_element_type=F32)
    return jnp.where(named > 0.0, rank, -1.0), gates


def slot_matrix(rank):
    rows, experts = rank.shape
    turned = rank.T
    slot = lax.broadcasted_iota(jnp.int32, (experts, CAP, rows), 1).astype(F32)
    return turned[:, None, :] == slot


def pack_rows_kernel(ids_ref, tokens_ref, out_ref):
    experts = out_ref.shape[0]
    rank, _ = membership(ids_ref[...], None, experts)
    chosen = slot_matrix(rank)
    pick = jnp.where(chosen, 1.0, 0.0).reshape(experts * CAP, -1).astype(BF)
    rows = jnp.dot(pick, tokens_ref[...], preferred_element_type=F32)
    out_ref[...] = rows.reshape(out_ref.shape).astype(BF)


def pack_back_kernel(ids_ref, weights_ref, cot_ref, out_ref):
    experts = out_ref.shape[0]
    rank, gates = membership(ids_ref[...], weights_ref[...], experts)
    chosen = slot_matrix(rank)
    pick = jnp.where(chosen, 1.0, 0.0).reshape(experts * CAP, -1).astype(BF)
    scale = jnp.sum(jnp.where(chosen, gates.T[:, None, :], 0.0), axis=2, keepdims=True)
    rows = jnp.dot(pick, cot_ref[...], preferred_element_type=F32)
    out_ref[...] = (rows.reshape(out_ref.shape) * scale).astype(BF)


def expand(values, experts):
    wide = experts * CAP
    col = lax.broadcasted_iota(jnp.int32, (experts, wide), 1)
    row = lax.broadcasted_iota(jnp.int32, (experts, wide), 0) * CAP
    spread = jnp.where((col >= row) & (col < row + CAP), 1.0, 0.0).astype(BF)
    return jnp.dot(values, spread, preferred_element_type=F32)


def slot_hits(rank, experts):
    wide = experts * CAP
    slot = lax.rem(lax.broadcasted_iota(jnp.int32, (rank.shape[0], wide), 1), CAP).astype(F32)
    return expand(rank.astype(BF), experts) == slot


def combine_out_kernel(ids_ref, weights_ref, back_ref, out_ref):
    experts = back_ref.shape[0] // CAP
    rank, gates = membership(ids_ref[...], weights_ref[...], experts)
    hits = slot_hits(rank, experts)
    back = back_ref[...]
    total = None
    rest = gates
    for _ in range(3):
        part = rest.astype(BF)
        rest = rest - part.astype(F32)
        term = jnp.dot(
            jnp.where(hits, expand(part, experts), 0.0).astype(BF), back, preferred_element_type=F32
        )
        total = term if total is None else total + term
    out_ref[...] = total.astype(BF)


def combine_grad_kernel(ids_ref, back_ref, out_ref):
    experts = back_ref.shape[0] // CAP
    rank, _ = membership(ids_ref[...], None, experts)
    pick = jnp.where(slot_hits(rank, experts), 1.0, 0.0).astype(BF)
    out_ref[...] = jnp.dot(pick, back_ref[...], preferred_element_type=F32).astype(BF)


def load_rows(ref):
    block = ref[:, 0].astype(F32)
    return block.reshape(-1, block.shape[-1]).astype(BF)


def load_lift(weights_ref, expert):
    return jnp.concatenate(
        [weights_ref[j, pl.ds(pl.multiple_of(expert * 128, 128), 128), :] for j in range(8)], axis=0
    )


def load_down(weights_ref, expert):
    base = weights_ref.shape[1] - 128
    return jnp.concatenate(
        [
            jnp.concatenate(
                [
                    weights_ref[j, base:, pl.ds(pl.multiple_of(expert * 384 + kb * 128, 128), 128)]
                    for j in range(8)
                ],
                axis=1,
            )
            for kb in range(3)
        ],
        axis=0,
    )


def forward_kernel(rows_ref, weights_ref, out_ref, act_ref, swish_ref, slope_ref):
    expert = pl.program_id(0)
    rows = load_rows(rows_ref)
    hidden = jnp.dot(rows, load_lift(weights_ref, expert), preferred_element_type=F32)
    ff = hidden.shape[1] // 2
    gate, up = hidden[:, :ff], hidden[:, ff:]
    sig = jax.nn.sigmoid(gate)
    swish = gate * sig
    act = (swish * up).astype(BF)
    act_ref[0] = act
    swish_ref[0] = swish
    slope_ref[0] = up * (sig * (1.0 + gate * (1.0 - sig)))
    out = jnp.dot(act, load_down(weights_ref, expert), preferred_element_type=F32)
    out_ref[:, 0] = out.reshape(out_ref.shape[0], CAP, -1).astype(BF)


def weight_grad_kernel(rows_ref, back_ref, act_ref, swish_ref, slope_ref, weights_ref, hid_ref, grad_ref):
    expert = pl.program_id(0)
    back = load_rows(back_ref)
    act_grad = lax.dot_general(
        back, load_down(weights_ref, expert), (((1,), (1,)), ((), ())), preferred_element_type=F32
    )
    hid = jnp.concatenate(
        [(act_grad * slope_ref[0]).astype(BF), (act_grad * swish_ref[0]).astype(BF)], axis=1
    )
    hid_ref[0] = hid
    first = (((0,), (0,)), ((), ()))
    down = lax.dot_general(act_ref[0], back, first, preferred_element_type=F32).astype(BF)
    lift = lax.dot_general(load_rows(rows_ref), hid, first, preferred_element_type=F32).astype(BF)
    base = weights_ref.shape[1] - 128
    for j in range(8):
        grad_ref[j, pl.ds(pl.multiple_of(expert * 128, 128), 128), :] = lift[j * 128 : (j + 1) * 128]
        for kb in range(3):
            grad_ref[j, base:, pl.ds(pl.multiple_of(expert * 384 + kb * 128, 128), 128)] = down[
                kb * 128 : (kb + 1) * 128, j * 128 : (j + 1) * 128
            ]


def input_grad_kernel(hid_ref, weights_ref, out_ref):
    expert = pl.program_id(0)
    grad = lax.dot_general(
        hid_ref[0], load_lift(weights_ref, expert), (((1,), (1,)), ((), ())), preferred_element_type=F32
    )
    out_ref[:, 0] = grad.reshape(out_ref.shape[0], CAP, -1).astype(BF)


def shards(tokens, expert_ids, combine_weights, lift_weights, down_weights, cotangent):
    tok, top = expert_ids.shape
    local, slice_rows, lift_width = lift_weights.shape
    ff = down_weights.shape[1]
    width = tokens.shape[1]
    owners = lax.axis_size("expert")
    groups = lax.axis_size("dp")
    experts = local * owners
    slots = owners * CAP
    bundle = local * slice_rows + 128
    vm = pl.BlockSpec(memory_space=pltpu.VMEM)

    joined = jnp.concatenate(
        [
            lift_weights.reshape(local * slice_rows, lift_width),
            down_weights.reshape(local, ff // 128, 128, 128).transpose(2, 0, 1, 3).reshape(128, lift_width),
        ],
        axis=0,
    )
    weights = lax.all_gather(joined, "dp")

    sent = jax.ShapeDtypeStruct((experts, CAP, width), BF)
    pack_flops = 2 * experts * CAP * tok * width
    send_rows = call(pack_rows_kernel, "pack_rows", sent, in_specs=[vm] * 2, flops=pack_flops, nbytes=8 << 20)(
        expert_ids, tokens
    )
    send_back = call(pack_back_kernel, "pack_back", sent, in_specs=[vm] * 3, flops=pack_flops, nbytes=8 << 20)(
        expert_ids, combine_weights, cotangent
    )
    buffer_shape = (owners, local, CAP, width)

    def exchange(x):
        return lax.all_to_all(x.reshape(buffer_shape), "expert", 0, 0, tiled=True)

    recv_rows = exchange(send_rows)
    recv_back = exchange(send_back)

    row_block = pl.BlockSpec((owners, 1, CAP, width), lambda e: (0, e, 0, 0))
    weight_block = pl.BlockSpec((groups, bundle, lift_width), lambda e: (0, 0, 0))
    half_block = pl.BlockSpec((1, slots, ff), lambda e: (e, 0, 0))
    hid_block = pl.BlockSpec((1, slots, 2 * ff), lambda e: (e, 0, 0))
    back_shape = jax.ShapeDtypeStruct(buffer_shape, BF)
    unit = 2 * local * slots * ff * width
    result, act, swish, slope = call(
        forward_kernel,
        "forward",
        [
            back_shape,
            jax.ShapeDtypeStruct((local, slots, ff), BF),
            jax.ShapeDtypeStruct((local, slots, ff), F32),
            jax.ShapeDtypeStruct((local, slots, ff), F32),
        ],
        grid=(local,),
        in_specs=[row_block, weight_block],
        out_specs=[row_block, half_block, half_block, half_block],
        flops=3 * unit,
        nbytes=16 << 20,
    )(recv_rows, weights)
    returned = exchange(result)
    recv_back, _ = lax.optimization_barrier((recv_back, result))
    hid, weight_grads = call(
        weight_grad_kernel,
        "weight_grad",
        [
            jax.ShapeDtypeStruct((local, slots, 2 * ff), BF),
            jax.ShapeDtypeStruct((groups, bundle, lift_width), BF),
        ],
        grid=(local,),
        in_specs=[row_block, row_block, half_block, half_block, half_block, weight_block],
        out_specs=[hid_block, weight_block],
        flops=4 * unit,
        nbytes=20 << 20,
    )(recv_rows, recv_back, act, swish, slope, weights)
    summed = lax.psum_scatter(weight_grads, "dp", scatter_dimension=0, tiled=False)
    input_grads = call(
        input_grad_kernel,
        "input_grad",
        back_shape,
        grid=(local,),
        in_specs=[hid_block, weight_block],
        out_specs=row_block,
        flops=2 * unit,
        nbytes=12 << 20,
    )(hid, weights)
    input_grads, returned = lax.optimization_barrier((input_grads, returned))
    returned_grads = exchange(input_grads)

    token_shape = jax.ShapeDtypeStruct((tok, width), BF)
    layer_output = call(
        combine_out_kernel, "combine_out", token_shape, in_specs=[vm] * 3, flops=3 * pack_flops, nbytes=4 << 20
    )(expert_ids, combine_weights, returned.reshape(experts * CAP, width))
    token_grads = call(
        combine_grad_kernel, "combine_grad", token_shape, in_specs=[vm] * 2, flops=pack_flops, nbytes=4 << 20
    )(expert_ids, returned_grads.reshape(experts * CAP, width))

    lift_grads = summed[: local * slice_rows].reshape(local, slice_rows, lift_width)
    down_grads = (
        summed[local * slice_rows :].reshape(128, local, ff // 128, 128).transpose(1, 2, 0, 3).reshape(local, ff, 128)
    )
    return (layer_output, token_grads, lift_grads, down_grads)


def solution(mesh):
    rows = P(("expert", "dp"), None)
    lift, down = P("expert", "dp", None), P("expert", None, "dp")
    return jax.shard_map(
        shards,
        mesh=mesh,
        in_specs=(rows, rows, rows, lift, down, rows),
        out_specs=(rows, rows, lift, down),
        check_vma=False,
    )
```

```python
import functools
import jax
import jax.numpy as jnp
from jax import lax
from jax.experimental import pallas as pl
from jax.experimental.pallas import tpu as pltpu
from jax.sharding import PartitionSpec as P

BF = jnp.bfloat16
F32 = jnp.float32
CAP = 24
SIDE = 4
CORES = 2
VMEM_LIMIT = 56 << 20


def call(kernel, name, out_shape, grid=None, in_specs=None, out_specs=None, scratch=(), flops=0, nbytes=0):
    full = pl.BlockSpec(memory_space=pltpu.VMEM)
    kwargs = {} if grid is None else {"grid": grid}
    return pl.pallas_call(
        kernel,
        name=name,
        out_shape=out_shape,
        in_specs=in_specs,
        out_specs=full if out_specs is None else out_specs,
        scratch_shapes=scratch,
        compiler_params=pltpu.CompilerParams(vmem_limit_bytes=VMEM_LIMIT),
        cost_estimate=pl.CostEstimate(flops=flops, transcendentals=0, bytes_accessed=nbytes),
        **kwargs,
    )


def split_parts(values, count):
    parts, rest = [], values
    for _ in range(count):
        part = rest.astype(BF).astype(F32)
        rest = rest - part
        parts.append(part)
    return parts


def bundle_kernel(ids_ref, weights_ref, tokens_ref, cot_ref, out_ref):
    tok, width = tokens_ref.shape
    out_ref[:tok] = tokens_ref[...]
    out_ref[tok : 2 * tok] = cot_ref[...]
    facts = [ids_ref[...].astype(F32)] + split_parts(weights_ref[...], 3)
    facts = jnp.concatenate(facts + [jnp.zeros((facts[0].shape[0], width - 4 * tok), F32)], axis=1)
    out_ref[2 * tok :] = jnp.concatenate([facts, jnp.zeros_like(facts)], axis=0).astype(BF)


def unbundle(ref, tok):
    facts = ref[ref.shape[0] - 16 :, : 4 * tok].astype(F32)[:8]
    pieces = [facts[:, n * tok : (n + 1) * tok] for n in range(4)]
    return pieces[0], (pieces[1] + pieces[2]) + pieces[3]


def membership(ids, weights, experts):
    top, rows = ids.shape
    expert = lax.broadcasted_iota(jnp.int32, (experts, rows), 0).astype(F32)
    named = jnp.zeros((experts, rows), F32)
    gates = jnp.zeros((experts, rows), F32)
    for k in range(top):
        hit = ids[k : k + 1, :] == expert
        named = jnp.where(hit, 1.0, named)
        if weights is not None:
            gates = jnp.where(hit, weights[k : k + 1, :], gates)
    before = (
        lax.broadcasted_iota(jnp.int32, (rows, rows), 0)
        < lax.broadcasted_iota(jnp.int32, (rows, rows), 1)
    ).astype(F32).astype(BF)
    rank = jnp.dot(named.astype(BF), before, preferred_element_type=F32)
    return jnp.where(named > 0.0, rank, -1.0), gates


def pack_kernel(first_ref, *refs):
    bundles, outs, (rank_ref, gate_ref) = refs[:4], refs[4:-2], refs[-2:]
    which = pl.program_id(0)
    tok = (bundles[0].shape[0] - 16) // 2
    found = []
    for q, bundle in enumerate(bundles):
        ids, weights = unbundle(bundle, tok)
        rank_ref[q], gate_ref[q] = membership(ids, weights, rank_ref.shape[1])
        rank = jnp.concatenate([rank_ref[q, pl.ds(first_ref[p], 2), :] for p in range(len(outs))], axis=0)
        gates = jnp.concatenate([gate_ref[q, pl.ds(first_ref[p], 2), :] for p in range(len(outs))], axis=0)
        slot = lax.broadcasted_iota(jnp.int32, (rank.shape[0], CAP, tok), 1).astype(F32)
        chosen = rank[:, None, :] == slot
        pick = jnp.where(chosen, 1.0, 0.0).reshape(-1, tok).astype(BF)
        scale = jnp.sum(jnp.where(chosen, gates[:, None, :], 0.0), axis=2, keepdims=True)
        scale = jnp.where(which == 0, 1.0, scale)
        data = bundle[pl.ds(pl.multiple_of(which * tok, tok), tok), :]
        rows = jnp.dot(pick, data, preferred_element_type=F32)
        found.append(rows.reshape(rank.shape[0], CAP, -1) * scale)
    for p, out in enumerate(outs):
        for e in range(2):
            out[0, e] = jnp.concatenate([rows[2 * p + e] for rows in found], axis=0).astype(BF)


def combine(first_ref, facts, chunks, rank_ref, gate_ref, weighted):
    tok = rank_ref.shape[2]
    sums = []
    for q, fact in enumerate(facts):
        ids, weights = unbundle(fact, tok)
        rank_ref[q], gate_ref[q] = membership(ids, weights, rank_ref.shape[1])
        rank = jnp.concatenate([rank_ref[q, pl.ds(first_ref[p], 2), :] for p in range(len(chunks))], axis=0)
        gates = jnp.concatenate([gate_ref[q, pl.ds(first_ref[p], 2), :] for p in range(len(chunks))], axis=0)
        slot = lax.broadcasted_iota(jnp.int32, (rank.shape[0], CAP, tok), 1).astype(F32)
        chosen = rank[:, None, :] == slot
        rows = jnp.concatenate([chunk[q] for chunk in chunks], axis=0)
        total = None
        for part in split_parts(gates, 3) if weighted else [jnp.ones_like(gates)]:
            pick = jnp.where(chosen, part[:, None, :], 0.0).reshape(-1, tok).astype(BF)
            term = lax.dot_general(pick, rows, (((0,), (0,)), ((), ())), preferred_element_type=F32)
            total = term if total is None else total + term
        sums.append(total)
    return sums


def combine_kernel(weighted, first_ref, *refs):
    facts, chunks, outs, tables = refs[:SIDE], refs[SIDE : -SIDE - 2], refs[-SIDE - 2 : -2], refs[-2:]
    for out, total in zip(outs, combine(first_ref, facts, chunks, *tables, weighted)):
        out[...] = total.astype(out.dtype)


def total_kernel(own_ref, *refs):
    total = own_ref[...]
    for ref in refs[:-1]:
        total = total + ref[...].astype(F32)
    refs[-1][...] = total.astype(BF)


def load_rows(chunks):
    return jnp.concatenate([chunk[0, 0] for chunk in chunks], axis=0)


def store_rows(rows, outs, hold_ref):
    expert = pl.program_id(0)

    @pl.when(expert == 0)
    def _():
        hold_ref[...] = rows

    @pl.when(expert == 1)
    def _():
        for p, out in enumerate(outs):
            for q in range(SIDE):
                part = pl.ds((p * SIDE + q) * CAP, CAP)
                low = (p * SIDE + q) * CAP
                out[q] = jnp.concatenate([hold_ref[part, :], rows[low : low + CAP]], axis=0).astype(BF)


def load_lift(weights_ref, expert):
    return jnp.concatenate(
        [weights_ref[j, pl.ds(pl.multiple_of(expert * 128, 128), 128), :] for j in range(8)], axis=0
    )


def load_down(weights_ref, expert):
    base = weights_ref.shape[1] - 128
    return jnp.concatenate(
        [
            jnp.concatenate(
                [
                    weights_ref[j, base:, pl.ds(pl.multiple_of(expert * 384 + kb * 128, 128), 128)]
                    for j in range(8)
                ],
                axis=1,
            )
            for kb in range(3)
        ],
        axis=0,
    )


def expert_kernel(*refs):
    chunks, (weights_ref, act_ref, hid_ref, grad_ref) = refs[:-4], refs[-4:]
    count = len(chunks) // 2
    expert = pl.program_id(0)
    rows, back = load_rows(chunks[:count]), load_rows(chunks[count:])
    hidden = jnp.dot(rows, load_lift(weights_ref, expert), preferred_element_type=F32)
    ff = hidden.shape[1] // 2
    gate, up = hidden[:, :ff], hidden[:, ff:]
    sig = jax.nn.sigmoid(gate)
    swish = gate * sig
    act = (swish * up).astype(BF)
    act_ref[0] = act
    act_grad = lax.dot_general(
        back, load_down(weights_ref, expert), (((1,), (1,)), ((), ())), preferred_element_type=F32
    )
    slope = sig * (1.0 + gate * (1.0 - sig))
    hid = jnp.concatenate([(act_grad * up * slope).astype(BF), (act_grad * swish).astype(BF)], axis=1)
    hid_ref[0] = hid
    first = (((0,), (0,)), ((), ()))
    down = lax.dot_general(act, back, first, preferred_element_type=F32).astype(BF)
    lift = lax.dot_general(rows, hid, first, preferred_element_type=F32).astype(BF)
    base = weights_ref.shape[1] - 128
    for j in range(8):
        grad_ref[j, pl.ds(pl.multiple_of(expert * 128, 128), 128), :] = lift[j * 128 : (j + 1) * 128]
        for kb in range(3):
            grad_ref[j, base:, pl.ds(pl.multiple_of(expert * 384 + kb * 128, 128), 128)] = down[
                kb * 128 : (kb + 1) * 128, j * 128 : (j + 1) * 128
            ]


def result_kernel(act_ref, weights_ref, *refs):
    out = jnp.dot(act_ref[0], load_down(weights_ref, pl.program_id(0)), preferred_element_type=F32)
    store_rows(out, refs[:-1], refs[-1])


def input_grad_kernel(hid_ref, weights_ref, *refs):
    grad = lax.dot_general(
        hid_ref[0],
        load_lift(weights_ref, pl.program_id(0)),
        (((1,), (1,)), ((), ())),
        preferred_element_type=F32,
    )
    store_rows(grad, refs[:-1], refs[-1])


def shards(tokens, expert_ids, combine_weights, lift_weights, down_weights, cotangent):
    tok, top = expert_ids.shape
    local, slice_rows, lift_width = lift_weights.shape
    ff = down_weights.shape[1]
    width = tokens.shape[1]
    owners = lax.axis_size("expert")
    groups = lax.axis_size("dp")
    experts = local * owners
    slots = owners * CAP
    bundle = local * slice_rows + 128
    vm = pl.BlockSpec(memory_space=pltpu.VMEM)

    joined = jnp.concatenate(
        [
            lift_weights.reshape(local * slice_rows, lift_width),
            down_weights.reshape(local, ff // 128, 128, 128).transpose(2, 0, 1, 3).reshape(128, lift_width),
        ],
        axis=0,
    )
    weights = lax.all_gather(joined, "dp")

    me = lax.axis_index("expert")
    near = SIDE * CORES

    def device(along, across, core):
        first = along if core == 0 else across
        second = across if core == 0 else along
        return (first % SIDE) * near + (second % SIDE) * CORES + core

    def place(n):
        x, y, c = n // near, n // CORES % SIDE, n % CORES
        return (x, y, c) if c == 0 else (y, x, c)

    def share_to(n, step):
        along, across, c = place(n)
        return device(along + step, across, c)

    def send_to(n, step, flip):
        x, y, c = n // near, n // CORES % SIDE, n % CORES
        x, y = (x, y + step) if c == 0 else (x + step, y)
        return (x % SIDE) * near + (y % SIDE) * CORES + (c + flip) % CORES

    def table(values):
        return jnp.asarray(values, jnp.int32)[me]

    hops = [(step, flip) for step in range(SIDE) for flip in range(CORES)]
    everyone = range(owners)
    first_expert = table([[local * send_to(n, *hop) for hop in hops] for n in everyone])

    ids, gates = expert_ids.T, combine_weights.T
    bundle_shape = jax.ShapeDtypeStruct((2 * tok + 16, width), BF)
    own = call(bundle_kernel, "bundle", bundle_shape, in_specs=[vm] * 4, nbytes=1 << 20)(
        ids, gates, tokens, cotangent
    )
    bundles = [own] + [
        lax.ppermute(own, "expert", [(n, share_to(n, q)) for n in everyone]) for q in range(1, SIDE)
    ]
    chunk_shape = jax.ShapeDtypeStruct((2, local, SIDE * CAP, width), BF)
    smem = pl.BlockSpec(memory_space=pltpu.SMEM)
    pack_flops = 2 * experts * CAP * tok * width
    table_scratch = pltpu.VMEM((SIDE, experts, tok), F32)
    packed = call(
        pack_kernel,
        "pack",
        [chunk_shape] * len(hops),
        grid=(2,),
        in_specs=[smem] + [vm] * SIDE,
        out_specs=[pl.BlockSpec((1, local, SIDE * CAP, width), lambda i: (i, 0, 0, 0))] * len(hops),
        scratch=[table_scratch, table_scratch],
        flops=2 * pack_flops,
        nbytes=16 << 20,
    )(first_expert, *bundles)
    chunks = [
        packed[p] if p == 0 else lax.ppermute(packed[p], "expert", [(n, send_to(n, *hop)) for n in everyone])
        for p, hop in enumerate(hops)
    ]

    count = len(hops)
    rows_blocks = [pl.BlockSpec((1, 1, SIDE * CAP, width), lambda e: (0, e, 0, 0))] * count
    back_blocks = [pl.BlockSpec((1, 1, SIDE * CAP, width), lambda e: (1, e, 0, 0))] * count
    weight_block = pl.BlockSpec((groups, bundle, lift_width), lambda e: (0, 0, 0))
    half_block = pl.BlockSpec((1, slots, ff), lambda e: (e, 0, 0))
    hid_block = pl.BlockSpec((1, slots, 2 * ff), lambda e: (e, 0, 0))
    back_shape = jax.ShapeDtypeStruct((SIDE, local * CAP, width), BF)
    back_block = pl.BlockSpec((SIDE, local * CAP, width), lambda e: (0, 0, 0))
    unit = 2 * local * slots * ff * width
    act, hid, weight_grads = call(
        expert_kernel,
        "expert",
        [
            jax.ShapeDtypeStruct((local, slots, ff), BF),
            jax.ShapeDtypeStruct((local, slots, 2 * ff), BF),
            jax.ShapeDtypeStruct((groups, bundle, lift_width), BF),
        ],
        grid=(local,),
        in_specs=rows_blocks + back_blocks + [weight_block],
        out_specs=[half_block, hid_block, weight_block],
        flops=6 * unit,
        nbytes=20 << 20,
    )(*chunks, *chunks, weights)
    summed = lax.psum_scatter(weight_grads, "dp", scatter_dimension=0, tiled=False)

    def returning(kernel, name, block, work, *operands):
        results = call(
            kernel,
            name,
            [back_shape] * count,
            grid=(local,),
            in_specs=[block, weight_block],
            out_specs=[back_block] * count,
            scratch=[pltpu.VMEM((slots, width), F32)],
            flops=work,
            nbytes=10 << 20,
        )(*operands)
        return [
            results[p] if p == 0 else lax.ppermute(results[p], "expert", [(send_to(n, *hop), n) for n in everyone])
            for p, hop in enumerate(hops)
        ]

    facts_block = pl.BlockSpec((16, width), lambda i: (2 * tok // 16, 0))
    whole_block = pl.BlockSpec((SIDE, local * CAP, width), lambda i: (0, 0, 0))
    token_shape = jax.ShapeDtypeStruct((tok, width), BF)
    token_block = pl.BlockSpec((tok, width), lambda i: (0, 0))

    def collected(weighted, name, results):
        sums = call(
            functools.partial(combine_kernel, weighted),
            name,
            [jax.ShapeDtypeStruct((tok, width), F32)] + [token_shape] * (SIDE - 1),
            grid=(1,),
            in_specs=[smem] + [facts_block] * SIDE + [whole_block] * count,
            out_specs=[token_block] * SIDE,
            scratch=[table_scratch, table_scratch],
            flops=pack_flops * (3 if weighted else 1),
            nbytes=4 << 20,
        )(first_expert, *bundles, *results)
        return list(sums[:1]) + [
            lax.ppermute(sums[q], "expert", [(share_to(n, q), n) for n in everyone]) for q in range(1, SIDE)
        ]

    def added(name, sums):
        return call(total_kernel, name, token_shape, in_specs=[vm] * SIDE, nbytes=1 << 20)(*sums)

    results = returning(result_kernel, "result", half_block, unit, act, weights)
    grads = returning(input_grad_kernel, "input_grad", hid_block, 2 * unit, hid, weights)
    result_sums = collected(True, "combine_out", results)
    grad_sums = collected(False, "combine_grad", grads)
    layer_output = added("total_out", result_sums)
    token_grads = added("total_grad", grad_sums)

    lift_grads = summed[: local * slice_rows].reshape(local, slice_rows, lift_width)
    down_grads = (
        summed[local * slice_rows :].reshape(128, local, ff // 128, 128).transpose(1, 2, 0, 3).reshape(local, ff, 128)
    )
    return (layer_output, token_grads, lift_grads, down_grads)


def solution(mesh):
    rows = P(("expert", "dp"), None)
    lift, down = P("expert", "dp", None), P("expert", None, "dp")
    return jax.shard_map(
        shards,
        mesh=mesh,
        in_specs=(rows, rows, rows, lift, down, rows),
        out_specs=(rows, rows, lift, down),
        check_vma=False,
    )
```

```python
import functools
import jax
import jax.numpy as jnp
from jax import lax
from jax.experimental import pallas as pl
from jax.experimental.pallas import tpu as pltpu
from jax.sharding import PartitionSpec as P

BF = jnp.bfloat16
F32 = jnp.float32
CAP = 24
SIDE = 4
CORES = 2
VMEM_LIMIT = 56 << 20


def call(kernel, name, out_shape, grid=None, in_specs=None, out_specs=None, scratch=(), flops=0, nbytes=0):
    full = pl.BlockSpec(memory_space=pltpu.VMEM)
    kwargs = {} if grid is None else {"grid": grid}
    return pl.pallas_call(
        kernel,
        name=name,
        out_shape=out_shape,
        in_specs=in_specs,
        out_specs=full if out_specs is None else out_specs,
        scratch_shapes=scratch,
        compiler_params=pltpu.CompilerParams(vmem_limit_bytes=VMEM_LIMIT),
        cost_estimate=pl.CostEstimate(flops=flops, transcendentals=0, bytes_accessed=nbytes),
        **kwargs,
    )


def split_parts(values, count):
    parts, rest = [], values
    for _ in range(count):
        part = rest.astype(BF).astype(F32)
        rest = rest - part
        parts.append(part)
    return parts


def down_pieces():
    return [(kb * 128 + h * 64, h * 384 + kb * 128) for kb in range(3) for h in range(2)]


def head_kernel(ids_ref, gates_ref, tokens_ref, cot_ref, lift_ref, down_ref, joined_ref, out_ref):
    for e in range(lift_ref.shape[0]):
        joined_ref[e, :128] = lift_ref[e]
        for row, col in down_pieces():
            joined_ref[e, 128:, col : col + 128] = down_ref[e, row : row + 64]
    tok, width = tokens_ref.shape
    out_ref[:tok] = tokens_ref[...]
    out_ref[tok : 2 * tok] = cot_ref[...]
    facts = [ids_ref[...].astype(F32)] + split_parts(gates_ref[...], 3)
    facts = jnp.concatenate(facts + [jnp.zeros((facts[0].shape[0], width - 4 * tok), F32)], axis=1)
    out_ref[2 * tok :] = jnp.concatenate([facts, jnp.zeros_like(facts)], axis=0).astype(BF)


def unbundle(ref, tok):
    facts = ref[ref.shape[0] - 16 :, : 4 * tok].astype(F32)[:8]
    pieces = [facts[:, n * tok : (n + 1) * tok] for n in range(4)]
    return pieces[0], (pieces[1] + pieces[2]) + pieces[3]


def membership(ids, weights, experts):
    top, rows = ids.shape
    expert = lax.broadcasted_iota(jnp.int32, (experts, rows), 0).astype(F32)
    named = jnp.zeros((experts, rows), F32)
    gates = jnp.zeros((experts, rows), F32)
    for k in range(top):
        hit = ids[k : k + 1, :] == expert
        named = jnp.where(hit, 1.0, named)
        gates = jnp.where(hit, weights[k : k + 1, :], gates)
    before = (
        lax.broadcasted_iota(jnp.int32, (rows, rows), 0)
        < lax.broadcasted_iota(jnp.int32, (rows, rows), 1)
    ).astype(F32).astype(BF)
    rank = jnp.dot(named.astype(BF), before, preferred_element_type=F32)
    return jnp.where(named > 0.0, rank, -1.0), gates


def slots(first_ref, fact_ref, count, rank_ref, gate_ref, q):
    tok = rank_ref.shape[2]
    ids, weights = unbundle(fact_ref, tok)
    rank_ref[q], gate_ref[q] = membership(ids, weights, rank_ref.shape[1])
    rank = jnp.concatenate([rank_ref[q, pl.ds(first_ref[p], 2), :] for p in range(count)], axis=0)
    gates = jnp.concatenate([gate_ref[q, pl.ds(first_ref[p], 2), :] for p in range(count)], axis=0)
    slot = lax.broadcasted_iota(jnp.int32, (rank.shape[0], CAP, tok), 1).astype(F32)
    return rank[:, None, :] == slot, gates


def pack_kernel(first_ref, *refs):
    bundles, outs, tables = refs[:SIDE], refs[SIDE:-2], refs[-2:]
    which = pl.program_id(0)
    tok = tables[0].shape[2]
    found = []
    for q, bundle in enumerate(bundles):
        chosen, gates = slots(first_ref, bundle, len(outs), *tables, q)
        pick = jnp.where(chosen, 1.0, 0.0).reshape(-1, tok).astype(BF)
        scale = jnp.sum(jnp.where(chosen, gates[:, None, :], 0.0), axis=2, keepdims=True)
        scale = jnp.where(which == 0, 1.0, scale)
        data = bundle[pl.ds(pl.multiple_of(which * tok, tok), tok), :]
        rows = jnp.dot(pick, data, preferred_element_type=F32)
        found.append(rows.reshape(-1, CAP, rows.shape[-1]) * scale)
    for p, out in enumerate(outs):
        for e in range(2):
            out[0, e] = jnp.concatenate([rows[2 * p + e] for rows in found], axis=0).astype(BF)


def plan_kernel(count, first_ref, *refs):
    facts, pick_ref, tables = refs[:SIDE], refs[-3], refs[-2:]
    tok = tables[0].shape[2]
    for q, fact in enumerate(facts):
        chosen, gates = slots(first_ref, fact, count, *tables, q)
        for i, weight in enumerate((gates, jnp.ones_like(gates))):
            for n, part in enumerate(split_parts(weight, 2)):
                pick = jnp.where(chosen, part[:, None, :], 0.0).reshape(-1, tok)
                pick_ref[i, q, n * tok : (n + 1) * tok] = pick.T.astype(BF)


def combine_kernel(places, pick_ref, *refs):
    chunks, outs = [refs[n] for n in places], refs[-SIDE:]
    for q, out in enumerate(outs):
        rows = jnp.concatenate([chunk[0, q] for chunk in chunks], axis=0)
        tok = out.shape[1]
        parts = jnp.dot(pick_ref[0, q], rows, preferred_element_type=F32)
        out[0] = (parts[:tok] + parts[tok:]).astype(out.dtype)


def final_kernel(sum_ref, own_ref, *refs):
    others, outs, (lift_ref, down_ref) = refs[: SIDE - 1], refs[SIDE - 1 : -2], refs[-2:]
    for e in range(lift_ref.shape[0]):
        lift_ref[e] = sum_ref[e, :128]
        for row, col in down_pieces():
            down_ref[e, row : row + 64] = sum_ref[e, 128:, col : col + 128]
    for which, out in enumerate(outs):
        total = own_ref[which]
        for ref in others:
            total = total + ref[which].astype(F32)
        out[...] = total.astype(BF)


def load_lift(weights_ref):
    return jnp.concatenate([weights_ref[j, 0, :128] for j in range(weights_ref.shape[0])], axis=0)


def load_down(weights_ref):
    return jnp.concatenate(
        [
            jnp.concatenate(
                [weights_ref[j, 0, 128:, col : col + 128] for j in range(weights_ref.shape[0])], axis=1
            )
            for _, col in down_pieces()
        ],
        axis=0,
    )


def store_rows(which, rows, outs, hold_ref):
    expert = pl.program_id(0)

    @pl.when(expert == 0)
    def _():
        hold_ref[which] = rows

    @pl.when(expert == 1)
    def _():
        for p, out in enumerate(outs):
            for q in range(SIDE):
                low = (p * SIDE + q) * CAP
                out[which, q] = jnp.concatenate(
                    [hold_ref[which, low : low + CAP, :], rows[low : low + CAP]], axis=0
                ).astype(BF)


def expert_kernel(count, *refs):
    chunks, weights_ref, outs = refs[:count], refs[count], refs[count + 2 : -2]
    grad_ref, hold_ref = refs[-2:]
    rows = jnp.concatenate([chunk[0, 0] for chunk in chunks], axis=0)
    back = jnp.concatenate([chunk[1, 0] for chunk in chunks], axis=0)
    lift_weights = load_lift(weights_ref)
    hidden = jnp.dot(rows, lift_weights, preferred_element_type=F32)
    ff = hidden.shape[1] // 2
    gate, up = hidden[:, :ff], hidden[:, ff:]
    sig = jax.nn.sigmoid(gate)
    swish = gate * sig
    act = (swish * up).astype(BF)
    down_weights = load_down(weights_ref)
    act_grad = lax.dot_general(back, down_weights, (((1,), (1,)), ((), ())), preferred_element_type=F32)
    slope = sig * (1.0 + gate * (1.0 - sig))
    hid = jnp.concatenate([(act_grad * up * slope).astype(BF), (act_grad * swish).astype(BF)], axis=1)
    first = (((0,), (0,)), ((), ()))
    down = lax.dot_general(act, back, first, preferred_element_type=F32).astype(BF)
    lift = lax.dot_general(rows, hid, first, preferred_element_type=F32).astype(BF)
    for j in range(grad_ref.shape[0]):
        grad_ref[j, 0, :128] = lift[j * 128 : (j + 1) * 128]
        for row, col in down_pieces():
            grad_ref[j, 0, 128:, col : col + 128] = down[row : row + 64, j * 128 : (j + 1) * 128]
    store_rows(0, jnp.dot(act, down_weights, preferred_element_type=F32), outs, hold_ref)
    grad = lax.dot_general(hid, lift_weights, (((1,), (1,)), ((), ())), preferred_element_type=F32)
    store_rows(1, grad, outs, hold_ref)


def shards(tokens, expert_ids, combine_weights, lift_weights, down_weights, cotangent):
    tok, top = expert_ids.shape
    local, slice_rows, lift_width = lift_weights.shape
    ff = down_weights.shape[1]
    width = tokens.shape[1]
    owners = lax.axis_size("expert")
    groups = lax.axis_size("dp")
    experts = local * owners
    filled = owners * CAP
    vm = pl.BlockSpec(memory_space=pltpu.VMEM)
    smem = pl.BlockSpec(memory_space=pltpu.SMEM)

    near = SIDE * CORES
    everyone = range(owners)

    def device(x, y, c):
        return (x % SIDE) * near + (y % SIDE) * CORES + c % CORES

    def share_to(n, step):
        x, y, c = n // near, n // CORES % SIDE, n % CORES
        return device(x + step, y, c) if c == 0 else device(x, y + step, c)

    def send_to(n, step, flip):
        x, y, c = n // near, n // CORES % SIDE, n % CORES
        return device(x, y + step, c + flip) if c == 0 else device(x + step, y, c + flip)

    def permute(x, target):
        return lax.ppermute(x, "expert", [(n, target(n)) for n in everyone])

    def restore(x, target):
        return lax.ppermute(x, "expert", [(target(n), n) for n in everyone])

    hops = [(step, flip) for step in range(SIDE) for flip in range(CORES)]
    count = len(hops)
    shared = [lambda n, q=q: share_to(n, q) for q in range(1, SIDE)]
    sends = [lambda n, hop=hop: send_to(n, *hop) for hop in hops[1:]]
    targets = jnp.asarray([[local * send_to(n, *hop) for hop in hops] for n in everyone], jnp.int32)
    first_expert = targets[lax.axis_index("expert")]

    joined, own = call(
        head_kernel,
        "head",
        [
            jax.ShapeDtypeStruct((local, slice_rows + 64, lift_width), BF),
            jax.ShapeDtypeStruct((2 * tok + 16, width), BF),
        ],
        in_specs=[vm] * 6,
        out_specs=[vm] * 2,
        nbytes=2 << 20,
    )(expert_ids.T, combine_weights.T, tokens, cotangent, lift_weights, down_weights)
    weights = lax.all_gather(joined, "dp")

    bundles = [own] + [permute(own, target) for target in shared]
    chunk_shape = jax.ShapeDtypeStruct((2, local, SIDE * CAP, width), BF)
    pack_flops = 2 * experts * CAP * tok * width
    table_scratch = pltpu.VMEM((SIDE, experts, tok), F32)
    packed = call(
        pack_kernel,
        "pack",
        [chunk_shape] * count,
        grid=(2,),
        in_specs=[smem] + [vm] * SIDE,
        out_specs=[pl.BlockSpec((1, local, SIDE * CAP, width), lambda i: (i, 0, 0, 0))] * count,
        scratch=[table_scratch, table_scratch],
        flops=2 * pack_flops,
        nbytes=16 << 20,
    )(first_expert, *bundles)
    chunks = list(packed[:1]) + [permute(x, target) for x, target in zip(packed[1:], sends)]
    slot_rows = local * count * CAP
    picks = call(
        functools.partial(plan_kernel, count),
        "plan",
        jax.ShapeDtypeStruct((2, SIDE, 2 * tok, slot_rows), BF),
        grid=(1,),
        in_specs=[smem]
        + [pl.BlockSpec((16, width), lambda i: (2 * tok // 16, 0))] * SIDE
        + [pl.BlockSpec(memory_space=pl.ANY)],
        out_specs=pl.BlockSpec((2, SIDE, 2 * tok, slot_rows), lambda i: (0, 0, 0, 0)),
        scratch=[table_scratch, table_scratch],
        nbytes=2 << 20,
    )(first_expert, *bundles, packed[0])

    weight_block = pl.BlockSpec((groups, 1, slice_rows + 64, lift_width), lambda e: (0, e, 0, 0))
    back_shape = jax.ShapeDtypeStruct((2, SIDE, local * CAP, width), BF)
    back_block = pl.BlockSpec((2, SIDE, local * CAP, width), lambda e: (0, 0, 0, 0))
    unit = 2 * local * filled * ff * width
    *returns, weight_grads = call(
        functools.partial(expert_kernel, count),
        "expert",
        [back_shape] * count
        + [jax.ShapeDtypeStruct((groups, local, slice_rows + 64, lift_width), BF)],
        grid=(local,),
        in_specs=[pl.BlockSpec((2, 1, SIDE * CAP, width), lambda e: (0, e, 0, 0))] * count
        + [weight_block, pl.BlockSpec(memory_space=pl.ANY)],
        out_specs=[back_block] * count + [weight_block],
        scratch=[pltpu.VMEM((2, filled, width), F32)],
        flops=9 * unit,
        nbytes=24 << 20,
    )(*chunks, weights, picks)
    summed = lax.psum_scatter(weight_grads, "dp", scatter_dimension=0, tiled=False)
    order = [0] + sorted(range(1, count), key=lambda p: (-hops[p][0] % SIDE, hops[p][1]))
    parts = [restore(returns[p], sends[p - 1]) if p else returns[0] for p in order]
    combining = functools.partial(combine_kernel, [order.index(p) for p in range(count)])
    sum_block = pl.BlockSpec((1, tok, width), lambda i: (i, 0, 0))
    sums = call(
        combining,
        "combine",
        [jax.ShapeDtypeStruct((2, tok, width), F32)] + [jax.ShapeDtypeStruct((2, tok, width), BF)] * (SIDE - 1),
        grid=(2,),
        in_specs=[pl.BlockSpec((1, SIDE, 2 * tok, slot_rows), lambda i: (i, 0, 0, 0))]
        + [pl.BlockSpec((1, SIDE, local * CAP, width), lambda i: (i, 0, 0, 0))] * count,
        out_specs=[sum_block] * SIDE,
        flops=4 * pack_flops,
        nbytes=10 << 20,
    )(picks, *parts)
    sums = list(sums[:1]) + [restore(x, target) for x, target in zip(sums[1:], shared)]
    token_shape = jax.ShapeDtypeStruct((tok, width), BF)
    return call(
        final_kernel,
        "final",
        [
            token_shape,
            token_shape,
            jax.ShapeDtypeStruct(lift_weights.shape, BF),
            jax.ShapeDtypeStruct(down_weights.shape, BF),
        ],
        in_specs=[vm] * (SIDE + 1),
        out_specs=[vm] * 4,
        nbytes=4 << 20,
    )(summed, *sums)


def solution(mesh):
    rows = P(("expert", "dp"), None)
    lift, down = P("expert", "dp", None), P("expert", None, "dp")
    return jax.shard_map(
        shards,
        mesh=mesh,
        in_specs=(rows, rows, rows, lift, down, rows),
        out_specs=(rows, rows, lift, down),
        check_vma=False,
    )
```

```python
import functools
import jax
import jax.numpy as jnp
from jax import lax
from jax.experimental import pallas as pl
from jax.experimental.pallas import tpu as pltpu
from jax.sharding import PartitionSpec as P

BF = jnp.bfloat16
F32 = jnp.float32
CAP = 24
SIDE = 4
CORES = 2


def call(kernel, name, out_shape, grid=None, in_specs=None, out_specs=None, scratch=(), flops=0, nbytes=0, vmem=16):
    full = pl.BlockSpec(memory_space=pltpu.VMEM)
    kwargs = {} if grid is None else {"grid": grid}
    return pl.pallas_call(
        kernel,
        name=name,
        out_shape=out_shape,
        in_specs=in_specs,
        out_specs=full if out_specs is None else out_specs,
        scratch_shapes=scratch,
        compiler_params=pltpu.CompilerParams(vmem_limit_bytes=vmem << 20),
        cost_estimate=pl.CostEstimate(flops=flops, transcendentals=0, bytes_accessed=nbytes),
        **kwargs,
    )


def split_parts(values, count):
    parts, rest = [], values
    for _ in range(count):
        part = rest.astype(BF).astype(F32)
        rest = rest - part
        parts.append(part)
    return parts


def down_pieces():
    return [(kb * 128 + h * 64, h * 384 + kb * 128) for kb in range(3) for h in range(2)]


def head_kernel(ids_ref, gates_ref, tokens_ref, cot_ref, lift_ref, down_ref, joined_ref, out_ref):
    for e in range(lift_ref.shape[0]):
        joined_ref[e, :128] = lift_ref[e]
        for row, col in down_pieces():
            joined_ref[e, 128:, col : col + 128] = down_ref[e, row : row + 64]
    tok, width = tokens_ref.shape
    out_ref[:tok] = tokens_ref[...]
    out_ref[tok : 2 * tok] = cot_ref[...]
    facts = [ids_ref[...].astype(F32)] + split_parts(gates_ref[...], 3)
    facts = jnp.concatenate(facts + [jnp.zeros((facts[0].shape[0], width - 4 * tok), F32)], axis=1)
    out_ref[2 * tok :] = jnp.concatenate([facts, jnp.zeros_like(facts)], axis=0).astype(BF)


def unbundle(ref, tok):
    facts = ref[ref.shape[0] - 16 :, : 4 * tok].astype(F32)[:8]
    pieces = [facts[:, n * tok : (n + 1) * tok] for n in range(4)]
    return pieces[0], (pieces[1] + pieces[2]) + pieces[3]


def membership(ids, weights, experts):
    top, rows = ids.shape
    expert = lax.broadcasted_iota(jnp.int32, (experts, rows), 0).astype(F32)
    named = jnp.zeros((experts, rows), F32)
    gates = jnp.zeros((experts, rows), F32)
    for k in range(top):
        hit = ids[k : k + 1, :] == expert
        named = jnp.where(hit, 1.0, named)
        gates = jnp.where(hit, weights[k : k + 1, :], gates)
    before = (
        lax.broadcasted_iota(jnp.int32, (rows, rows), 0)
        < lax.broadcasted_iota(jnp.int32, (rows, rows), 1)
    ).astype(F32).astype(BF)
    rank = jnp.dot(named.astype(BF), before, preferred_element_type=F32)
    return jnp.where(named > 0.0, rank, -1.0), gates


def slots(first_ref, fact_ref, count, rank_ref, gate_ref, q):
    tok = rank_ref.shape[2]
    ids, weights = unbundle(fact_ref, tok)
    rank_ref[q], gate_ref[q] = membership(ids, weights, rank_ref.shape[1])
    rank = jnp.concatenate([rank_ref[q, pl.ds(first_ref[p], 2), :] for p in range(count)], axis=0)
    gates = jnp.concatenate([gate_ref[q, pl.ds(first_ref[p], 2), :] for p in range(count)], axis=0)
    slot = lax.broadcasted_iota(jnp.int32, (rank.shape[0], CAP, tok), 1).astype(F32)
    return rank[:, None, :] == slot, gates


def pack_kernel(first_ref, *refs):
    bundles, outs, tables = refs[:SIDE], refs[SIDE:-2], refs[-2:]
    tok = tables[0].shape[2]
    sent, back = [], []
    for q, bundle in enumerate(bundles):
        chosen, gates = slots(first_ref, bundle, len(outs), *tables, q)
        pick = jnp.where(chosen, 1.0, 0.0).reshape(-1, tok).astype(BF)
        scale = jnp.sum(jnp.where(chosen, gates[:, None, :], 0.0), axis=2, keepdims=True)
        rows = jnp.dot(pick, bundle[:tok], preferred_element_type=F32)
        sent.append(rows.reshape(-1, CAP, rows.shape[-1]))
        rows = jnp.dot(pick, bundle[tok : 2 * tok], preferred_element_type=F32)
        back.append(rows.reshape(-1, CAP, rows.shape[-1]) * scale)
    for p, out in enumerate(outs):
        for which, found in enumerate((sent, back)):
            for e in range(2):
                out[which, e] = jnp.concatenate([rows[2 * p + e] for rows in found], axis=0).astype(BF)


def plan_kernel(count, first_ref, *refs):
    facts, pick_ref, tables = refs[:SIDE], refs[-3], refs[-2:]
    tok = tables[0].shape[2]
    for q, fact in enumerate(facts):
        chosen, gates = slots(first_ref, fact, count, *tables, q)
        for i, weight in enumerate((gates, jnp.ones_like(gates))):
            for n, part in enumerate(split_parts(weight, 2)):
                pick = jnp.where(chosen, part[:, None, :], 0.0).reshape(-1, tok)
                pick_ref[i, q, n * tok : (n + 1) * tok] = pick.T.astype(BF)


def combine_kernel(places, pick_ref, *refs):
    chunks, outs = [refs[n] for n in places], refs[-SIDE:]
    for q, out in enumerate(outs):
        rows = jnp.concatenate([chunk[0, q] for chunk in chunks], axis=0)
        tok = out.shape[1]
        parts = jnp.dot(pick_ref[0, q], rows, preferred_element_type=F32)
        out[0] = (parts[:tok] + parts[tok:]).astype(out.dtype)


def final_kernel(sum_ref, own_ref, *refs):
    others, outs, (lift_ref, down_ref) = refs[: SIDE - 1], refs[SIDE - 1 : -2], refs[-2:]
    for e in range(lift_ref.shape[0]):
        lift_ref[e] = sum_ref[e, :128]
        for row, col in down_pieces():
            down_ref[e, row : row + 64] = sum_ref[e, 128:, col : col + 128]
    for which, out in enumerate(outs):
        total = own_ref[which]
        for ref in others:
            total = total + ref[which].astype(F32)
        out[...] = total.astype(BF)


def load_lift(weights_ref):
    return jnp.concatenate([weights_ref[j, 0, :128] for j in range(weights_ref.shape[0])], axis=0)


def load_down(weights_ref):
    return jnp.concatenate(
        [
            jnp.concatenate(
                [weights_ref[j, 0, 128:, col : col + 128] for j in range(weights_ref.shape[0])], axis=1
            )
            for _, col in down_pieces()
        ],
        axis=0,
    )


def store_rows(which, rows, outs):
    for p, out in enumerate(outs):
        for q in range(SIDE):
            low = (p * SIDE + q) * CAP
            out[which, q, 0] = rows[low : low + CAP].astype(BF)


def expert_kernel(count, *refs):
    chunks, weights_ref, outs = refs[:count], refs[count], refs[count + 2 : -1]
    grad_ref = refs[-1]
    rows = jnp.concatenate([chunk[0, 0] for chunk in chunks], axis=0)
    back = jnp.concatenate([chunk[1, 0] for chunk in chunks], axis=0)
    lift_weights = load_lift(weights_ref)
    hidden = jnp.dot(rows, lift_weights, preferred_element_type=F32)
    ff = hidden.shape[1] // 2
    gate, up = hidden[:, :ff], hidden[:, ff:]
    sig = jax.nn.sigmoid(gate)
    swish = gate * sig
    act = (swish * up).astype(BF)
    down_weights = load_down(weights_ref)
    act_grad = lax.dot_general(back, down_weights, (((1,), (1,)), ((), ())), preferred_element_type=F32)
    slope = sig * (1.0 + gate * (1.0 - sig))
    hid = jnp.concatenate([(act_grad * up * slope).astype(BF), (act_grad * swish).astype(BF)], axis=1)
    first = (((0,), (0,)), ((), ()))
    down = lax.dot_general(act, back, first, preferred_element_type=F32).astype(BF)
    lift = lax.dot_general(rows, hid, first, preferred_element_type=F32).astype(BF)
    for j in range(grad_ref.shape[0]):
        grad_ref[j, 0, :128] = lift[j * 128 : (j + 1) * 128]
        for row, col in down_pieces():
            grad_ref[j, 0, 128:, col : col + 128] = down[row : row + 64, j * 128 : (j + 1) * 128]
    store_rows(0, jnp.dot(act, down_weights, preferred_element_type=F32), outs)
    grad = lax.dot_general(hid, lift_weights, (((1,), (1,)), ((), ())), preferred_element_type=F32)
    store_rows(1, grad, outs)


def shards(tokens, expert_ids, combine_weights, lift_weights, down_weights, cotangent):
    tok, top = expert_ids.shape
    local, slice_rows, lift_width = lift_weights.shape
    ff = down_weights.shape[1]
    width = tokens.shape[1]
    owners = lax.axis_size("expert")
    groups = lax.axis_size("dp")
    experts = local * owners
    filled = owners * CAP
    vm = pl.BlockSpec(memory_space=pltpu.VMEM)
    smem = pl.BlockSpec(memory_space=pltpu.SMEM)

    near = SIDE * CORES
    everyone = range(owners)

    def device(x, y, c):
        return (x % SIDE) * near + (y % SIDE) * CORES + c % CORES

    def share_to(n, step):
        x, y, c = n // near, n // CORES % SIDE, n % CORES
        return device(x + step, y, c) if c == 0 else device(x, y + step, c)

    def send_to(n, step, flip):
        x, y, c = n // near, n // CORES % SIDE, n % CORES
        return device(x, y + step, c + flip) if c == 0 else device(x + step, y, c + flip)

    def permute(x, target):
        return lax.ppermute(x, "expert", [(n, target(n)) for n in everyone])

    def onchip(x):
        return pltpu.with_memory_space_constraint(x, pltpu.VMEM)

    def restore(x, target):
        return lax.ppermute(x, "expert", [(target(n), n) for n in everyone])

    hops = [(step, flip) for step in range(SIDE) for flip in range(CORES)]
    count = len(hops)
    shared = [lambda n, q=q: share_to(n, q) for q in range(1, SIDE)]
    sends = [lambda n, hop=hop: send_to(n, *hop) for hop in hops[1:]]
    targets = jnp.asarray([[local * send_to(n, *hop) for hop in hops] for n in everyone], jnp.int32)
    first_expert = targets[lax.axis_index("expert")]

    joined, own = call(
        head_kernel,
        "head",
        [
            jax.ShapeDtypeStruct((local, slice_rows + 64, lift_width), BF),
            jax.ShapeDtypeStruct((2 * tok + 16, width), BF),
        ],
        in_specs=[vm] * 6,
        out_specs=[vm] * 2,
        nbytes=2 << 20,
        vmem=56,
    )(expert_ids.T, combine_weights.T, tokens, cotangent, lift_weights, down_weights)
    weights = lax.all_gather(joined, "dp")

    bundles = [own] + [permute(own, target) for target in shared]
    chunk_shape = jax.ShapeDtypeStruct((2, local, SIDE * CAP, width), BF)
    pack_flops = 2 * experts * CAP * tok * width
    table_scratch = pltpu.VMEM((SIDE, experts, tok), F32)
    packed = call(
        pack_kernel,
        "pack",
        [pltpu.VMEM(chunk_shape.shape, BF)] * count,
        in_specs=[smem] + [vm] * SIDE,
        out_specs=[vm] * count,
        scratch=[table_scratch, table_scratch],
        flops=2 * pack_flops,
        vmem=32,
        nbytes=16 << 20,
    )(first_expert, *[onchip(x) for x in bundles])
    chunks = list(packed[:1]) + [permute(x, target) for x, target in zip(packed[1:], sends)]
    slot_rows = local * count * CAP
    picks = call(
        functools.partial(plan_kernel, count),
        "plan",
        jax.ShapeDtypeStruct((2, SIDE, 2 * tok, slot_rows), BF),
        grid=(1,),
        in_specs=[smem]
        + [pl.BlockSpec((16, width), lambda i: (2 * tok // 16, 0))] * SIDE
        + [pl.BlockSpec(memory_space=pl.ANY)],
        out_specs=pl.BlockSpec((2, SIDE, 2 * tok, slot_rows), lambda i: (0, 0, 0, 0)),
        scratch=[table_scratch, table_scratch],
        nbytes=2 << 20,
    )(first_expert, *bundles, packed[0])

    weight_block = pl.BlockSpec((groups, 1, slice_rows + 64, lift_width), lambda e: (0, e, 0, 0))
    back_shape = jax.ShapeDtypeStruct((2, SIDE, local, CAP, width), BF)
    back_block = pl.BlockSpec((2, SIDE, 1, CAP, width), lambda e: (0, 0, e, 0, 0))
    unit = 2 * local * filled * ff * width
    *returns, weight_grads = call(
        functools.partial(expert_kernel, count),
        "expert",
        [back_shape] * count
        + [jax.ShapeDtypeStruct((groups, local, slice_rows + 64, lift_width), BF)],
        grid=(local,),
        in_specs=[pl.BlockSpec((2, 1, SIDE * CAP, width), lambda e: (0, e, 0, 0))] * count
        + [weight_block, pl.BlockSpec(memory_space=pl.ANY)],
        out_specs=[back_block] * count + [weight_block],
        flops=9 * unit,
        vmem=56,
        nbytes=24 << 20,
    )(*chunks, weights, picks)
    summed = lax.psum_scatter(weight_grads, "dp", scatter_dimension=0, tiled=False)
    returns = [x.reshape(2, SIDE, local * CAP, width) for x in returns]
    order = [0] + sorted(range(1, count), key=lambda p: (-hops[p][0] % SIDE, hops[p][1]))
    parts = [restore(returns[p], sends[p - 1]) if p else returns[0] for p in order]
    combining = functools.partial(combine_kernel, [order.index(p) for p in range(count)])
    sum_block = pl.BlockSpec((1, tok, width), lambda i: (i, 0, 0))
    sums = call(
        combining,
        "combine",
        [jax.ShapeDtypeStruct((2, tok, width), F32)] + [jax.ShapeDtypeStruct((2, tok, width), BF)] * (SIDE - 1),
        grid=(2,),
        in_specs=[pl.BlockSpec((1, SIDE, 2 * tok, slot_rows), lambda i: (i, 0, 0, 0))]
        + [pl.BlockSpec((1, SIDE, local * CAP, width), lambda i: (i, 0, 0, 0))] * count,
        out_specs=[sum_block] * SIDE,
        flops=4 * pack_flops,
        nbytes=10 << 20,
    )(picks, *parts)
    sums = list(sums[:1]) + [restore(x, target) for x, target in zip(sums[1:], shared)]
    token_shape = jax.ShapeDtypeStruct((tok, width), BF)
    return call(
        final_kernel,
        "final",
        [
            token_shape,
            token_shape,
            jax.ShapeDtypeStruct(lift_weights.shape, BF),
            jax.ShapeDtypeStruct(down_weights.shape, BF),
        ],
        in_specs=[vm] * (SIDE + 1),
        out_specs=[vm] * 4,
        nbytes=4 << 20,
    )(summed, *sums)


def solution(mesh):
    rows = P(("expert", "dp"), None)
    lift, down = P("expert", "dp", None), P("expert", None, "dp")
    return jax.shard_map(
        shards,
        mesh=mesh,
        in_specs=(rows, rows, rows, lift, down, rows),
        out_specs=(rows, rows, lift, down),
        check_vma=False,
    )
```

```python
import functools
import jax
import jax.numpy as jnp
from jax import lax
from jax.experimental import pallas as pl
from jax.experimental.pallas import tpu as pltpu
from jax.sharding import PartitionSpec as P

BF = jnp.bfloat16
F32 = jnp.float32
CAP = 24
SIDE = 4
CORES = 2


def call(kernel, name, out_shape, grid=None, in_specs=None, out_specs=None, scratch=(), flops=0, nbytes=0, vmem=16):
    full = pl.BlockSpec(memory_space=pltpu.VMEM)
    kwargs = {} if grid is None else {"grid": grid}
    return pl.pallas_call(
        kernel,
        name=name,
        out_shape=out_shape,
        in_specs=in_specs,
        out_specs=full if out_specs is None else out_specs,
        scratch_shapes=scratch,
        compiler_params=pltpu.CompilerParams(vmem_limit_bytes=vmem << 20),
        cost_estimate=pl.CostEstimate(flops=flops, transcendentals=0, bytes_accessed=nbytes),
        **kwargs,
    )


def split_parts(values, count):
    parts, rest = [], values
    for _ in range(count):
        part = rest.astype(BF).astype(F32)
        rest = rest - part
        parts.append(part)
    return parts


def down_pieces():
    return [(kb * 128 + h * 64, h * 384 + kb * 128) for kb in range(3) for h in range(2)]


def head_kernel(ids_ref, gates_ref, tokens_ref, cot_ref, lift_ref, down_ref, joined_ref, out_ref):
    for e in range(lift_ref.shape[0]):
        joined_ref[e, :128] = lift_ref[e]
        for row, col in down_pieces():
            joined_ref[e, 128:, col : col + 128] = down_ref[e, row : row + 64]
    tok, width = tokens_ref.shape
    out_ref[:tok] = tokens_ref[...]
    out_ref[tok : 2 * tok] = cot_ref[...]
    facts = [ids_ref[...].astype(F32)] + split_parts(gates_ref[...], 3)
    facts = jnp.concatenate(facts + [jnp.zeros((facts[0].shape[0], width - 4 * tok), F32)], axis=1)
    out_ref[2 * tok :] = jnp.concatenate([facts, jnp.zeros_like(facts)], axis=0).astype(BF)


def unbundle(ref, tok):
    facts = ref[ref.shape[0] - 16 :, : 4 * tok].astype(F32)[:8]
    pieces = [facts[:, n * tok : (n + 1) * tok] for n in range(4)]
    return pieces[0], (pieces[1] + pieces[2]) + pieces[3]


def membership(ids, weights, experts):
    top, rows = ids.shape
    expert = lax.broadcasted_iota(jnp.int32, (experts, rows), 0).astype(F32)
    named = jnp.zeros((experts, rows), F32)
    gates = jnp.zeros((experts, rows), F32)
    for k in range(top):
        hit = ids[k : k + 1, :] == expert
        named = jnp.where(hit, 1.0, named)
        gates = jnp.where(hit, weights[k : k + 1, :], gates)
    before = (
        lax.broadcasted_iota(jnp.int32, (rows, rows), 0)
        < lax.broadcasted_iota(jnp.int32, (rows, rows), 1)
    ).astype(F32).astype(BF)
    rank = jnp.dot(named.astype(BF), before, preferred_element_type=F32)
    return jnp.where(named > 0.0, rank, -1.0), gates


def slots(first_ref, fact_ref, count, rank_ref, gate_ref, q):
    tok = rank_ref.shape[2]
    ids, weights = unbundle(fact_ref, tok)
    rank_ref[q], gate_ref[q] = membership(ids, weights, rank_ref.shape[1])
    rank = jnp.concatenate([rank_ref[q, pl.ds(first_ref[p], 2), :] for p in range(count)], axis=0)
    gates = jnp.concatenate([gate_ref[q, pl.ds(first_ref[p], 2), :] for p in range(count)], axis=0)
    slot = lax.broadcasted_iota(jnp.int32, (rank.shape[0], CAP, tok), 1).astype(F32)
    return rank[:, None, :] == slot, gates


def pack_kernel(first_ref, *refs):
    bundles, outs, tables = refs[:SIDE], refs[SIDE:-2], refs[-2:]
    tok = tables[0].shape[2]
    sent, back = [], []
    for q, bundle in enumerate(bundles):
        chosen, gates = slots(first_ref, bundle, len(outs), *tables, q)
        pick = jnp.where(chosen, 1.0, 0.0).reshape(-1, tok).astype(BF)
        scale = jnp.sum(jnp.where(chosen, gates[:, None, :], 0.0), axis=2, keepdims=True)
        rows = jnp.dot(pick, bundle[:tok], preferred_element_type=F32)
        sent.append(rows.reshape(-1, CAP, rows.shape[-1]))
        rows = jnp.dot(pick, bundle[tok : 2 * tok], preferred_element_type=F32)
        back.append(rows.reshape(-1, CAP, rows.shape[-1]) * scale)
    for p, out in enumerate(outs):
        for which, found in enumerate((sent, back)):
            for e in range(2):
                out[which, e] = jnp.concatenate([rows[2 * p + e] for rows in found], axis=0).astype(BF)


def plan_kernel(count, first_ref, *refs):
    facts, pick_ref, tables = refs[:SIDE], refs[-3], refs[-2:]
    tok = tables[0].shape[2]
    for q, fact in enumerate(facts):
        chosen, gates = slots(first_ref, fact, count, *tables, q)
        for i, weight in enumerate((gates, jnp.ones_like(gates))):
            for n, part in enumerate(split_parts(weight, 2)):
                pick = jnp.where(chosen, part[:, None, :], 0.0).reshape(-1, tok)
                pick_ref[i, q, n * tok : (n + 1) * tok] = pick.T.astype(BF)


def combine_kernel(places, pick_ref, *refs):
    chunks, outs = [refs[n] for n in places], refs[-SIDE:]
    for q, out in enumerate(outs):
        rows = jnp.concatenate([chunk[0, q] for chunk in chunks], axis=0)
        tok = out.shape[1]
        parts = jnp.dot(pick_ref[0, q], rows, preferred_element_type=F32)
        out[0] = (parts[:tok] + parts[tok:]).astype(out.dtype)


def final_kernel(sum_ref, own_ref, *refs):
    others, outs, (lift_ref, down_ref) = refs[: SIDE - 1], refs[SIDE - 1 : -2], refs[-2:]
    for e in range(lift_ref.shape[0]):
        lift_ref[e] = sum_ref[e, :128]
        for row, col in down_pieces():
            down_ref[e, row : row + 64] = sum_ref[e, 128:, col : col + 128]
    for which, out in enumerate(outs):
        total = own_ref[which]
        for ref in others:
            total = total + ref[which].astype(F32)
        out[...] = total.astype(BF)


def load_lift(weights_ref):
    return jnp.concatenate([weights_ref[j, 0, :128] for j in range(weights_ref.shape[0])], axis=0)


def load_down(weights_ref):
    return jnp.concatenate(
        [
            jnp.concatenate(
                [weights_ref[j, 0, 128:, col : col + 128] for j in range(weights_ref.shape[0])], axis=1
            )
            for _, col in down_pieces()
        ],
        axis=0,
    )


def store_rows(which, rows, outs):
    for p, out in enumerate(outs):
        for q in range(SIDE):
            low = (p * SIDE + q) * CAP
            out[which, q, 0] = rows[low : low + CAP].astype(BF)


def expert_kernel(count, *refs):
    chunks, weights_ref, outs = refs[:count], refs[count], refs[count + 2 : -1]
    grad_ref = refs[-1]
    rows = jnp.concatenate([chunk[0, 0] for chunk in chunks], axis=0)
    back = jnp.concatenate([chunk[1, 0] for chunk in chunks], axis=0)
    lift_weights = load_lift(weights_ref)
    hidden = jnp.dot(rows, lift_weights, preferred_element_type=F32)
    ff = hidden.shape[1] // 2
    gate, up = hidden[:, :ff], hidden[:, ff:]
    sig = jax.nn.sigmoid(gate)
    swish = gate * sig
    act = (swish * up).astype(BF)
    down_weights = load_down(weights_ref)
    act_grad = lax.dot_general(back, down_weights, (((1,), (1,)), ((), ())), preferred_element_type=F32)
    slope = sig * (1.0 + gate * (1.0 - sig))
    hid = jnp.concatenate([(act_grad * up * slope).astype(BF), (act_grad * swish).astype(BF)], axis=1)
    first = (((0,), (0,)), ((), ()))
    down = lax.dot_general(act, back, first, preferred_element_type=F32).astype(BF)
    lift = lax.dot_general(rows, hid, first, preferred_element_type=F32).astype(BF)
    for j in range(grad_ref.shape[0]):
        grad_ref[j, 0, :128] = lift[j * 128 : (j + 1) * 128]
        for row, col in down_pieces():
            grad_ref[j, 0, 128:, col : col + 128] = down[row : row + 64, j * 128 : (j + 1) * 128]
    store_rows(0, jnp.dot(act, down_weights, preferred_element_type=F32), outs)
    grad = lax.dot_general(hid, lift_weights, (((1,), (1,)), ((), ())), preferred_element_type=F32)
    store_rows(1, grad, outs)


def shards(tokens, expert_ids, combine_weights, lift_weights, down_weights, cotangent):
    tok, top = expert_ids.shape
    local, slice_rows, lift_width = lift_weights.shape
    ff = down_weights.shape[1]
    width = tokens.shape[1]
    owners = lax.axis_size("expert")
    groups = lax.axis_size("dp")
    experts = local * owners
    filled = owners * CAP
    vm = pl.BlockSpec(memory_space=pltpu.VMEM)
    smem = pl.BlockSpec(memory_space=pltpu.SMEM)

    near = SIDE * CORES
    everyone = range(owners)

    def device(x, y, c):
        return (x % SIDE) * near + (y % SIDE) * CORES + c % CORES

    def share_to(n, step):
        x, y, c = n // near, n // CORES % SIDE, n % CORES
        return device(x + step, y, c) if c == 0 else device(x, y + step, c)

    def send_to(n, step, flip):
        x, y, c = n // near, n // CORES % SIDE, n % CORES
        return device(x, y + step, c + flip) if c == 0 else device(x + step, y, c + flip)

    def permute(x, target):
        return lax.ppermute(x, "expert", [(n, target(n)) for n in everyone])

    def onchip(x):
        return pltpu.with_memory_space_constraint(x, pltpu.VMEM)

    def offchip(x):
        return pltpu.with_memory_space_constraint(x, pltpu.HBM)

    def restore(x, target):
        return lax.ppermute(x, "expert", [(target(n), n) for n in everyone])

    hops = [(step, flip) for step in range(SIDE) for flip in range(CORES)]
    count = len(hops)
    shared = [lambda n, q=q: share_to(n, q) for q in range(1, SIDE)]
    sends = [lambda n, hop=hop: send_to(n, *hop) for hop in hops[1:]]
    targets = jnp.asarray([[local * send_to(n, *hop) for hop in hops] for n in everyone], jnp.int32)
    first_expert = targets[lax.axis_index("expert")]

    joined, own = call(
        head_kernel,
        "head",
        [
            jax.ShapeDtypeStruct((local, slice_rows + 64, lift_width), BF),
            jax.ShapeDtypeStruct((2 * tok + 16, width), BF),
        ],
        in_specs=[vm] * 6,
        out_specs=[vm] * 2,
        nbytes=2 << 20,
        vmem=56,
    )(expert_ids.T, combine_weights.T, tokens, cotangent, lift_weights, down_weights)
    weights = lax.all_gather(joined, "dp")

    bundles = [own] + [permute(own, target) for target in shared]
    chunk_shape = jax.ShapeDtypeStruct((2, local, SIDE * CAP, width), BF)
    pack_flops = 2 * experts * CAP * tok * width
    table_scratch = pltpu.VMEM((SIDE, experts, tok), F32)
    packed = call(
        pack_kernel,
        "pack",
        [pltpu.VMEM(chunk_shape.shape, BF)] * count,
        in_specs=[smem] + [vm] * SIDE,
        out_specs=[vm] * count,
        scratch=[table_scratch, table_scratch],
        flops=2 * pack_flops,
        vmem=32,
        nbytes=16 << 20,
    )(first_expert, offchip(own), *[onchip(x) for x in bundles[1:]])
    chunks = list(packed[:1]) + [permute(x, target) for x, target in zip(packed[1:], sends)]
    slot_rows = local * count * CAP
    picks = call(
        functools.partial(plan_kernel, count),
        "plan",
        jax.ShapeDtypeStruct((2, SIDE, 2 * tok, slot_rows), BF),
        grid=(1,),
        in_specs=[smem]
        + [pl.BlockSpec((16, width), lambda i: (2 * tok // 16, 0))] * SIDE
        + [pl.BlockSpec(memory_space=pl.ANY)],
        out_specs=pl.BlockSpec((2, SIDE, 2 * tok, slot_rows), lambda i: (0, 0, 0, 0)),
        scratch=[table_scratch, table_scratch],
        nbytes=2 << 20,
    )(first_expert, *bundles, packed[0])

    weight_block = pl.BlockSpec((groups, 1, slice_rows + 64, lift_width), lambda e: (0, e, 0, 0))
    back_shape = jax.ShapeDtypeStruct((2, SIDE, local, CAP, width), BF)
    back_block = pl.BlockSpec((2, SIDE, 1, CAP, width), lambda e: (0, 0, e, 0, 0))
    unit = 2 * local * filled * ff * width
    *returns, weight_grads = call(
        functools.partial(expert_kernel, count),
        "expert",
        [back_shape] * count
        + [jax.ShapeDtypeStruct((groups, local, slice_rows + 64, lift_width), BF)],
        grid=(local,),
        in_specs=[pl.BlockSpec((2, 1, SIDE * CAP, width), lambda e: (0, e, 0, 0))] * count
        + [weight_block, pl.BlockSpec(memory_space=pl.ANY)],
        out_specs=[back_block] * count + [weight_block],
        flops=9 * unit,
        vmem=56,
        nbytes=24 << 20,
    )(*[offchip(x) for x in chunks], weights, picks)
    summed = lax.psum_scatter(weight_grads, "dp", scatter_dimension=0, tiled=False)
    returns = [x.reshape(2, SIDE, local * CAP, width) for x in returns]
    order = [0] + sorted(range(1, count), key=lambda p: (-hops[p][0] % SIDE, hops[p][1]))
    parts = [restore(returns[p], sends[p - 1]) if p else returns[0] for p in order]
    combining = functools.partial(combine_kernel, [order.index(p) for p in range(count)])
    sum_block = pl.BlockSpec((1, tok, width), lambda i: (i, 0, 0))
    sums = call(
        combining,
        "combine",
        [jax.ShapeDtypeStruct((2, tok, width), F32)] + [jax.ShapeDtypeStruct((2, tok, width), BF)] * (SIDE - 1),
        grid=(2,),
        in_specs=[pl.BlockSpec((1, SIDE, 2 * tok, slot_rows), lambda i: (i, 0, 0, 0))]
        + [pl.BlockSpec((1, SIDE, local * CAP, width), lambda i: (i, 0, 0, 0))] * count,
        out_specs=[sum_block] * SIDE,
        flops=4 * pack_flops,
        nbytes=10 << 20,
    )(picks, *parts)
    sums = list(sums[:1]) + [restore(x, target) for x, target in zip(sums[1:], shared)]
    token_shape = jax.ShapeDtypeStruct((tok, width), BF)
    return call(
        final_kernel,
        "final",
        [
            token_shape,
            token_shape,
            jax.ShapeDtypeStruct(lift_weights.shape, BF),
            jax.ShapeDtypeStruct(down_weights.shape, BF),
        ],
        in_specs=[vm] * (SIDE + 1),
        out_specs=[vm] * 4,
        nbytes=4 << 20,
    )(offchip(summed), *sums)


def solution(mesh):
    rows = P(("expert", "dp"), None)
    lift, down = P("expert", "dp", None), P("expert", None, "dp")
    return jax.shard_map(
        shards,
        mesh=mesh,
        in_specs=(rows, rows, rows, lift, down, rows),
        out_specs=(rows, rows, lift, down),
        check_vma=False,
    )
```

```python
import functools
import jax
import jax.numpy as jnp
from jax import lax
from jax.experimental import pallas as pl
from jax.experimental.pallas import tpu as pltpu
from jax.sharding import PartitionSpec as P

BF = jnp.bfloat16
F32 = jnp.float32
CAP = 24
SIDE = 4
CORES = 2
SPARE = 8


def call(kernel, name, out_shape, grid=None, in_specs=None, out_specs=None, scratch=(), flops=0, nbytes=0, vmem=16):
    full = pl.BlockSpec(memory_space=pltpu.VMEM)
    kwargs = {} if grid is None else {"grid": grid}
    return pl.pallas_call(
        kernel,
        name=name,
        out_shape=out_shape,
        in_specs=in_specs,
        out_specs=full if out_specs is None else out_specs,
        scratch_shapes=scratch,
        compiler_params=pltpu.CompilerParams(vmem_limit_bytes=vmem << 20),
        cost_estimate=pl.CostEstimate(flops=flops, transcendentals=0, bytes_accessed=nbytes),
        **kwargs,
    )


def split_parts(values, count):
    parts, rest = [], values
    for _ in range(count):
        part = rest.astype(BF).astype(F32)
        rest = rest - part
        parts.append(part)
    return parts


def down_pieces():
    return [(kb * 128 + h * 64, h * 384 + kb * 128) for kb in range(3) for h in range(2)]


def head_kernel(ids_ref, gates_ref, tokens_ref, cot_ref, lift_ref, down_ref, joined_ref, out_ref):
    for e in range(lift_ref.shape[0]):
        joined_ref[e, :128] = lift_ref[e]
        for row, col in down_pieces():
            joined_ref[e, 128:, col : col + 128] = down_ref[e, row : row + 64]
    tok, width = tokens_ref.shape
    out_ref[:tok] = tokens_ref[...]
    out_ref[tok : 2 * tok] = cot_ref[...]
    facts = [ids_ref[...].astype(F32)] + split_parts(gates_ref[...], 3)
    facts = jnp.concatenate(facts + [jnp.zeros((facts[0].shape[0], width - 4 * tok), F32)], axis=1)
    out_ref[2 * tok :] = jnp.concatenate([facts, jnp.zeros_like(facts)], axis=0).astype(BF)


def unbundle(ref, tok):
    facts = ref[ref.shape[0] - 16 :, : 4 * tok].astype(F32)[:8]
    pieces = [facts[:, n * tok : (n + 1) * tok] for n in range(4)]
    return pieces[0], (pieces[1] + pieces[2]) + pieces[3]


def membership(ids, weights, experts):
    top, rows = ids.shape
    expert = lax.broadcasted_iota(jnp.int32, (experts, rows), 0).astype(F32)
    named = jnp.zeros((experts, rows), F32)
    gates = jnp.zeros((experts, rows), F32)
    for k in range(top):
        hit = ids[k : k + 1, :] == expert
        named = jnp.where(hit, 1.0, named)
        gates = jnp.where(hit, weights[k : k + 1, :], gates)
    before = (
        lax.broadcasted_iota(jnp.int32, (rows, rows), 0)
        < lax.broadcasted_iota(jnp.int32, (rows, rows), 1)
    ).astype(F32).astype(BF)
    rank = jnp.dot(named.astype(BF), before, preferred_element_type=F32)
    return jnp.where(named > 0.0, rank, -1.0), gates


def slots(first_ref, fact_ref, count, rank_ref, gate_ref, q):
    tok = rank_ref.shape[2]
    ids, weights = unbundle(fact_ref, tok)
    experts = rank_ref.shape[1] - SPARE
    rank_ref[q, :experts], gate_ref[q, :experts] = membership(ids, weights, experts)
    rank = jnp.concatenate([rank_ref[q, pl.ds(first_ref[p], 2), :] for p in range(count)], axis=0)
    gates = jnp.concatenate([gate_ref[q, pl.ds(first_ref[p], 2), :] for p in range(count)], axis=0)
    slot = lax.broadcasted_iota(jnp.int32, (rank.shape[0], CAP, tok), 1).astype(F32)
    return rank[:, None, :] == slot, gates


def pack_kernel(first_ref, *refs):
    bundles, outs, tables = refs[:SIDE], refs[SIDE:-2], refs[-2:]
    tok = tables[0].shape[2]
    sent, back = [], []
    for q, bundle in enumerate(bundles):
        chosen, gates = slots(first_ref, bundle, len(outs), *tables, q)
        pick = jnp.where(chosen, 1.0, 0.0).reshape(-1, tok).astype(BF)
        scale = jnp.sum(jnp.where(chosen, gates[:, None, :], 0.0), axis=2, keepdims=True)
        rows = jnp.dot(pick, bundle[:tok], preferred_element_type=F32)
        sent.append(rows.reshape(-1, CAP, rows.shape[-1]))
        rows = jnp.dot(pick, bundle[tok : 2 * tok], preferred_element_type=F32)
        back.append(rows.reshape(-1, CAP, rows.shape[-1]) * scale)
    for p, out in enumerate(outs):
        for which, found in enumerate((sent, back)):
            for e in range(2):
                out[which, e] = jnp.concatenate([rows[2 * p + e] for rows in found], axis=0).astype(BF)


def plan_kernel(count, first_ref, *refs):
    facts, pick_ref, tables = refs[:SIDE], refs[-3], refs[-2:]
    tok = tables[0].shape[2]
    for q, fact in enumerate(facts):
        chosen, gates = slots(first_ref, fact, count, *tables, q)
        for i, weight in enumerate((gates, jnp.ones_like(gates))):
            for n, part in enumerate(split_parts(weight, 2)):
                pick = jnp.where(chosen, part[:, None, :], 0.0).reshape(-1, tok)
                pick_ref[i, q, n * tok : (n + 1) * tok] = pick.T.astype(BF)


def combine_kernel(places, pick_ref, *refs):
    chunks, outs = [refs[n] for n in places], refs[-SIDE:]
    for q, out in enumerate(outs):
        rows = jnp.concatenate([chunk[0, q] for chunk in chunks], axis=0)
        tok = out.shape[1]
        parts = jnp.dot(pick_ref[0, q], rows, preferred_element_type=F32)
        out[0] = (parts[:tok] + parts[tok:]).astype(out.dtype)


def final_kernel(sum_ref, own_ref, *refs):
    others, outs, (lift_ref, down_ref) = refs[: SIDE - 1], refs[SIDE - 1 : -2], refs[-2:]
    for e in range(lift_ref.shape[0]):
        lift_ref[e] = sum_ref[e, :128]
        for row, col in down_pieces():
            down_ref[e, row : row + 64] = sum_ref[e, 128:, col : col + 128]
    for which, out in enumerate(outs):
        total = own_ref[which]
        for ref in others:
            total = total + ref[which].astype(F32)
        out[...] = total.astype(BF)


def load_lift(weights_ref):
    return jnp.concatenate([weights_ref[j, 0, :128] for j in range(weights_ref.shape[0])], axis=0)


def load_down(weights_ref):
    return jnp.concatenate(
        [
            jnp.concatenate(
                [weights_ref[j, 0, 128:, col : col + 128] for j in range(weights_ref.shape[0])], axis=1
            )
            for _, col in down_pieces()
        ],
        axis=0,
    )


def store_rows(which, rows, outs):
    for p, out in enumerate(outs):
        for q in range(SIDE):
            low = (p * SIDE + q) * CAP
            out[which, q, 0] = rows[low : low + CAP].astype(BF)


def expert_kernel(count, *refs):
    chunks, weights_ref, outs = refs[:count], refs[count], refs[count + 2 : -1]
    grad_ref = refs[-1]
    rows = jnp.concatenate([chunk[0, 0] for chunk in chunks], axis=0)
    back = jnp.concatenate([chunk[1, 0] for chunk in chunks], axis=0)
    lift_weights = load_lift(weights_ref)
    hidden = jnp.dot(rows, lift_weights, preferred_element_type=F32)
    ff = hidden.shape[1] // 2
    gate, up = hidden[:, :ff], hidden[:, ff:]
    sig = jax.nn.sigmoid(gate)
    swish = gate * sig
    act = (swish * up).astype(BF)
    down_weights = load_down(weights_ref)
    act_grad = lax.dot_general(back, down_weights, (((1,), (1,)), ((), ())), preferred_element_type=F32)
    slope = sig * (1.0 + gate * (1.0 - sig))
    hid = jnp.concatenate([(act_grad * up * slope).astype(BF), (act_grad * swish).astype(BF)], axis=1)
    first = (((0,), (0,)), ((), ()))
    down = lax.dot_general(act, back, first, preferred_element_type=F32).astype(BF)
    lift = lax.dot_general(rows, hid, first, preferred_element_type=F32).astype(BF)
    for j in range(grad_ref.shape[0]):
        grad_ref[j, 0, :128] = lift[j * 128 : (j + 1) * 128]
        for row, col in down_pieces():
            grad_ref[j, 0, 128:, col : col + 128] = down[row : row + 64, j * 128 : (j + 1) * 128]
    store_rows(0, jnp.dot(act, down_weights, preferred_element_type=F32), outs)
    grad = lax.dot_general(hid, lift_weights, (((1,), (1,)), ((), ())), preferred_element_type=F32)
    store_rows(1, grad, outs)


def shards(tokens, expert_ids, combine_weights, lift_weights, down_weights, cotangent):
    tok, top = expert_ids.shape
    local, slice_rows, lift_width = lift_weights.shape
    ff = down_weights.shape[1]
    width = tokens.shape[1]
    owners = lax.axis_size("expert")
    groups = lax.axis_size("dp")
    experts = local * owners
    filled = owners * CAP
    vm = pl.BlockSpec(memory_space=pltpu.VMEM)
    smem = pl.BlockSpec(memory_space=pltpu.SMEM)

    near = SIDE * CORES
    everyone = range(owners)

    def device(x, y, c):
        return (x % SIDE) * near + (y % SIDE) * CORES + c % CORES

    def share_to(n, step):
        x, y, c = n // near, n // CORES % SIDE, n % CORES
        return device(x + step, y, c) if c == 0 else device(x, y + step, c)

    def send_to(n, step, flip):
        x, y, c = n // near, n // CORES % SIDE, n % CORES
        return device(x, y + step, c + flip) if c == 0 else device(x + step, y, c + flip)

    def permute(x, target):
        return lax.ppermute(x, "expert", [(n, target(n)) for n in everyone])

    def onchip(x):
        return pltpu.with_memory_space_constraint(x, pltpu.VMEM)

    def offchip(x):
        return pltpu.with_memory_space_constraint(x, pltpu.HBM)

    def restore(x, target):
        return lax.ppermute(x, "expert", [(target(n), n) for n in everyone])

    hops = [(step, flip) for step in range(SIDE) for flip in range(CORES)]
    count = len(hops)
    shared = [lambda n, q=q: share_to(n, q) for q in range(1, SIDE)]
    sends = [lambda n, hop=hop: send_to(n, *hop) for hop in hops[1:]]
    targets = jnp.asarray([[local * send_to(n, *hop) for hop in hops] for n in everyone], jnp.int32)
    first_expert = targets[lax.axis_index("expert")]

    joined, own = call(
        head_kernel,
        "head",
        [
            jax.ShapeDtypeStruct((local, slice_rows + 64, lift_width), BF),
            jax.ShapeDtypeStruct((2 * tok + 16, width), BF),
        ],
        in_specs=[vm] * 6,
        out_specs=[vm] * 2,
        nbytes=2 << 20,
        vmem=56,
    )(expert_ids.T, combine_weights.T, tokens, cotangent, lift_weights, down_weights)
    weights = lax.all_gather(joined, "dp")

    bundles = [own] + [permute(own, target) for target in shared]
    chunk_shape = jax.ShapeDtypeStruct((2, local, SIDE * CAP, width), BF)
    pack_flops = 2 * experts * CAP * tok * width
    table_scratch = pltpu.VMEM((SIDE, experts + SPARE, tok), F32)
    packed = call(
        pack_kernel,
        "pack",
        [pltpu.VMEM(chunk_shape.shape, BF)] * count,
        in_specs=[smem] + [vm] * SIDE,
        out_specs=[vm] * count,
        scratch=[table_scratch, table_scratch],
        flops=2 * pack_flops,
        vmem=32,
        nbytes=16 << 20,
    )(first_expert, offchip(own), *[onchip(x) for x in bundles[1:]])
    chunks = list(packed[:1]) + [permute(x, target) for x, target in zip(packed[1:], sends)]
    slot_rows = local * count * CAP
    picks = call(
        functools.partial(plan_kernel, count),
        "plan",
        jax.ShapeDtypeStruct((2, SIDE, 2 * tok, slot_rows), BF),
        grid=(1,),
        in_specs=[smem]
        + [pl.BlockSpec((16, width), lambda i: (2 * tok // 16, 0))] * SIDE
        + [pl.BlockSpec(memory_space=pl.ANY)],
        out_specs=pl.BlockSpec((2, SIDE, 2 * tok, slot_rows), lambda i: (0, 0, 0, 0)),
        scratch=[table_scratch, table_scratch],
        nbytes=2 << 20,
    )(first_expert, *bundles, packed[0])

    weight_block = pl.BlockSpec((groups, 1, slice_rows + 64, lift_width), lambda e: (0, e, 0, 0))
    back_shape = jax.ShapeDtypeStruct((2, SIDE, local, CAP, width), BF)
    back_block = pl.BlockSpec((2, SIDE, 1, CAP, width), lambda e: (0, 0, e, 0, 0))
    unit = 2 * local * filled * ff * width
    *returns, weight_grads = call(
        functools.partial(expert_kernel, count),
        "expert",
        [back_shape] * count
        + [jax.ShapeDtypeStruct((groups, local, slice_rows + 64, lift_width), BF)],
        grid=(local,),
        in_specs=[pl.BlockSpec((2, 1, SIDE * CAP, width), lambda e: (0, e, 0, 0))] * count
        + [weight_block, pl.BlockSpec(memory_space=pl.ANY)],
        out_specs=[back_block] * count + [weight_block],
        flops=9 * unit,
        vmem=56,
        nbytes=24 << 20,
    )(*[offchip(x) for x in chunks], weights, picks)
    summed = lax.psum_scatter(weight_grads, "dp", scatter_dimension=0, tiled=False)
    returns = [x.reshape(2, SIDE, local * CAP, width) for x in returns]
    order = [0] + sorted(range(1, count), key=lambda p: (-hops[p][0] % SIDE, hops[p][1]))
    parts = [restore(returns[p], sends[p - 1]) if p else returns[0] for p in order]
    combining = functools.partial(combine_kernel, [order.index(p) for p in range(count)])
    sum_block = pl.BlockSpec((1, tok, width), lambda i: (i, 0, 0))
    sums = call(
        combining,
        "combine",
        [jax.ShapeDtypeStruct((2, tok, width), F32)] + [jax.ShapeDtypeStruct((2, tok, width), BF)] * (SIDE - 1),
        grid=(2,),
        in_specs=[pl.BlockSpec((1, SIDE, 2 * tok, slot_rows), lambda i: (i, 0, 0, 0))]
        + [pl.BlockSpec((1, SIDE, local * CAP, width), lambda i: (i, 0, 0, 0))] * count,
        out_specs=[sum_block] * SIDE,
        flops=4 * pack_flops,
        nbytes=10 << 20,
    )(picks, *parts)
    sums = list(sums[:1]) + [restore(x, target) for x, target in zip(sums[1:], shared)]
    token_shape = jax.ShapeDtypeStruct((tok, width), BF)
    return call(
        final_kernel,
        "final",
        [
            token_shape,
            token_shape,
            jax.ShapeDtypeStruct(lift_weights.shape, BF),
            jax.ShapeDtypeStruct(down_weights.shape, BF),
        ],
        in_specs=[vm] * (SIDE + 1),
        out_specs=[vm] * 4,
        nbytes=4 << 20,
    )(offchip(summed), *sums)


def solution(mesh):
    rows = P(("expert", "dp"), None)
    lift, down = P("expert", "dp", None), P("expert", None, "dp")
    return jax.shard_map(
        shards,
        mesh=mesh,
        in_specs=(rows, rows, rows, lift, down, rows),
        out_specs=(rows, rows, lift, down),
        check_vma=False,
    )
```

```python
import functools
import jax
import jax.numpy as jnp
from jax import lax
from jax.experimental import pallas as pl
from jax.experimental.pallas import tpu as pltpu
from jax.sharding import PartitionSpec as P

BF = jnp.bfloat16
F32 = jnp.float32
CAP = 24
SIDE = 4
CORES = 2
SPARE = 8


def call(kernel, name, out_shape, grid=None, in_specs=None, out_specs=None, scratch=(), flops=0, nbytes=0, vmem=16):
    full = pl.BlockSpec(memory_space=pltpu.VMEM)
    kwargs = {} if grid is None else {"grid": grid}
    return pl.pallas_call(
        kernel,
        name=name,
        out_shape=out_shape,
        in_specs=in_specs,
        out_specs=full if out_specs is None else out_specs,
        scratch_shapes=scratch,
        compiler_params=pltpu.CompilerParams(vmem_limit_bytes=vmem << 20),
        cost_estimate=pl.CostEstimate(flops=flops, transcendentals=0, bytes_accessed=nbytes),
        **kwargs,
    )


def split_parts(values, count):
    parts, rest = [], values
    for _ in range(count):
        part = rest.astype(BF).astype(F32)
        rest = rest - part
        parts.append(part)
    return parts


def down_pieces():
    return [(kb * 128 + h * 64, h * 384 + kb * 128) for kb in range(3) for h in range(2)]


def head_kernel(ids_ref, gates_ref, tokens_ref, cot_ref, lift_ref, down_ref, joined_ref, out_ref):
    for e in range(lift_ref.shape[0]):
        joined_ref[e, :128] = lift_ref[e]
        for row, col in down_pieces():
            joined_ref[e, 128:, col : col + 128] = down_ref[e, row : row + 64]
    tok, width = tokens_ref.shape
    out_ref[:tok] = tokens_ref[...]
    out_ref[tok : 2 * tok] = cot_ref[...]
    facts = [ids_ref[...].astype(F32)] + split_parts(gates_ref[...], 3)
    facts = jnp.concatenate(facts + [jnp.zeros((facts[0].shape[0], width - 4 * tok), F32)], axis=1)
    out_ref[2 * tok :] = jnp.concatenate([facts, jnp.zeros_like(facts)], axis=0).astype(BF)


def unbundle(ref, tok):
    facts = ref[ref.shape[0] - 16 :, : 4 * tok].astype(F32)[:8]
    pieces = [facts[:, n * tok : (n + 1) * tok] for n in range(4)]
    return pieces[0], (pieces[1] + pieces[2]) + pieces[3]


def membership(ids, weights, experts):
    top, rows = ids.shape
    expert = lax.broadcasted_iota(jnp.int32, (experts, rows), 0).astype(F32)
    named = jnp.zeros((experts, rows), F32)
    gates = jnp.zeros((experts, rows), F32)
    for k in range(top):
        hit = ids[k : k + 1, :] == expert
        named = jnp.where(hit, 1.0, named)
        gates = jnp.where(hit, weights[k : k + 1, :], gates)
    before = (
        lax.broadcasted_iota(jnp.int32, (rows, rows), 0)
        < lax.broadcasted_iota(jnp.int32, (rows, rows), 1)
    ).astype(F32).astype(BF)
    rank = jnp.dot(named.astype(BF), before, preferred_element_type=F32)
    return jnp.where(named > 0.0, rank, -1.0), gates


def slots(first_ref, fact_ref, count, rank_ref, gate_ref, q):
    tok = rank_ref.shape[2]
    ids, weights = unbundle(fact_ref, tok)
    experts = rank_ref.shape[1] - SPARE
    rank_ref[q, :experts], gate_ref[q, :experts] = membership(ids, weights, experts)
    rank = jnp.concatenate([rank_ref[q, pl.ds(first_ref[p], 2), :] for p in range(count)], axis=0)
    gates = jnp.concatenate([gate_ref[q, pl.ds(first_ref[p], 2), :] for p in range(count)], axis=0)
    slot = lax.broadcasted_iota(jnp.int32, (rank.shape[0], CAP, tok), 1).astype(F32)
    return rank[:, None, :] == slot, gates


def pack_kernel(first_ref, *refs):
    bundles, outs, tables = refs[:SIDE], refs[SIDE:-2], refs[-2:]
    tok = tables[0].shape[2]
    sent, back = [], []
    for q, bundle in enumerate(bundles):
        chosen, gates = slots(first_ref, bundle, len(outs), *tables, q)
        pick = jnp.where(chosen, 1.0, 0.0).reshape(-1, tok).astype(BF)
        scale = jnp.sum(jnp.where(chosen, gates[:, None, :], 0.0), axis=2, keepdims=True)
        rows = jnp.dot(pick, bundle[:tok], preferred_element_type=F32)
        sent.append(rows.reshape(-1, CAP, rows.shape[-1]))
        rows = jnp.dot(pick, bundle[tok : 2 * tok], preferred_element_type=F32)
        back.append(rows.reshape(-1, CAP, rows.shape[-1]) * scale)
    for p, out in enumerate(outs):
        for which, found in enumerate((sent, back)):
            for e in range(2):
                out[which, e] = jnp.concatenate([rows[2 * p + e] for rows in found], axis=0).astype(BF)


def plan_kernel(count, first_ref, *refs):
    facts, pick_ref, tables = refs[:SIDE], refs[-3], refs[-2:]
    tok = tables[0].shape[2]
    for q, fact in enumerate(facts):
        chosen, gates = slots(first_ref, fact, count, *tables, q)
        for i, weight in enumerate((gates, jnp.ones_like(gates))):
            for n, part in enumerate(split_parts(weight, 2)):
                pick = jnp.where(chosen, part[:, None, :], 0.0).reshape(-1, tok)
                pick_ref[i, q, n * tok : (n + 1) * tok] = pick.T.astype(BF)


def combine_kernel(places, pick_ref, *refs):
    chunks, outs = [refs[n] for n in places], refs[-SIDE:]
    for q, out in enumerate(outs):
        rows = jnp.concatenate([chunk[0, q] for chunk in chunks], axis=0)
        tok = out.shape[1]
        parts = jnp.dot(pick_ref[0, q], rows, preferred_element_type=F32)
        out[0] = (parts[:tok] + parts[tok:]).astype(out.dtype)


def split_kernel(sum_ref, lift_ref, down_ref):
    for e in range(lift_ref.shape[0]):
        lift_ref[e] = sum_ref[e, :128]
        for row, col in down_pieces():
            down_ref[e, row : row + 64] = sum_ref[e, 128:, col : col + 128]


def total_kernel(own_ref, *refs):
    others, outs = refs[: SIDE - 1], refs[SIDE - 1 :]
    for which, out in enumerate(outs):
        total = own_ref[which]
        for ref in others:
            total = total + ref[which].astype(F32)
        out[...] = total.astype(BF)


def load_lift(weights_ref):
    return jnp.concatenate([weights_ref[j, 0, :128] for j in range(weights_ref.shape[0])], axis=0)


def load_down(weights_ref):
    return jnp.concatenate(
        [
            jnp.concatenate(
                [weights_ref[j, 0, 128:, col : col + 128] for j in range(weights_ref.shape[0])], axis=1
            )
            for _, col in down_pieces()
        ],
        axis=0,
    )


def store_rows(which, rows, outs):
    for p, out in enumerate(outs):
        for q in range(SIDE):
            low = (p * SIDE + q) * CAP
            out[which, q, 0] = rows[low : low + CAP].astype(BF)


def expert_kernel(count, *refs):
    chunks, weights_ref, outs = refs[:count], refs[count], refs[count + 2 : -1]
    grad_ref = refs[-1]
    rows = jnp.concatenate([chunk[0, 0] for chunk in chunks], axis=0)
    back = jnp.concatenate([chunk[1, 0] for chunk in chunks], axis=0)
    lift_weights = load_lift(weights_ref)
    hidden = jnp.dot(rows, lift_weights, preferred_element_type=F32)
    ff = hidden.shape[1] // 2
    gate, up = hidden[:, :ff], hidden[:, ff:]
    sig = jax.nn.sigmoid(gate)
    swish = gate * sig
    act = (swish * up).astype(BF)
    down_weights = load_down(weights_ref)
    act_grad = lax.dot_general(back, down_weights, (((1,), (1,)), ((), ())), preferred_element_type=F32)
    slope = sig * (1.0 + gate * (1.0 - sig))
    hid = jnp.concatenate([(act_grad * up * slope).astype(BF), (act_grad * swish).astype(BF)], axis=1)
    first = (((0,), (0,)), ((), ()))
    down = lax.dot_general(act, back, first, preferred_element_type=F32).astype(BF)
    lift = lax.dot_general(rows, hid, first, preferred_element_type=F32).astype(BF)
    for j in range(grad_ref.shape[0]):
        grad_ref[j, 0, :128] = lift[j * 128 : (j + 1) * 128]
        for row, col in down_pieces():
            grad_ref[j, 0, 128:, col : col + 128] = down[row : row + 64, j * 128 : (j + 1) * 128]
    store_rows(0, jnp.dot(act, down_weights, preferred_element_type=F32), outs)
    grad = lax.dot_general(hid, lift_weights, (((1,), (1,)), ((), ())), preferred_element_type=F32)
    store_rows(1, grad, outs)


def shards(tokens, expert_ids, combine_weights, lift_weights, down_weights, cotangent):
    tok, top = expert_ids.shape
    local, slice_rows, lift_width = lift_weights.shape
    ff = down_weights.shape[1]
    width = tokens.shape[1]
    owners = lax.axis_size("expert")
    groups = lax.axis_size("dp")
    experts = local * owners
    filled = owners * CAP
    vm = pl.BlockSpec(memory_space=pltpu.VMEM)
    smem = pl.BlockSpec(memory_space=pltpu.SMEM)

    near = SIDE * CORES
    everyone = range(owners)

    def device(x, y, c):
        return (x % SIDE) * near + (y % SIDE) * CORES + c % CORES

    def share_to(n, step):
        x, y, c = n // near, n // CORES % SIDE, n % CORES
        return device(x + step, y, c) if c == 0 else device(x, y + step, c)

    def send_to(n, step, flip):
        x, y, c = n // near, n // CORES % SIDE, n % CORES
        return device(x, y + step, c + flip) if c == 0 else device(x + step, y, c + flip)

    def permute(x, target):
        return lax.ppermute(x, "expert", [(n, target(n)) for n in everyone])

    def onchip(x):
        return pltpu.with_memory_space_constraint(x, pltpu.VMEM)

    def offchip(x):
        return pltpu.with_memory_space_constraint(x, pltpu.HBM)

    def restore(x, target):
        return lax.ppermute(x, "expert", [(target(n), n) for n in everyone])

    hops = [(step, flip) for step in range(SIDE) for flip in range(CORES)]
    count = len(hops)
    shared = [lambda n, q=q: share_to(n, q) for q in range(1, SIDE)]
    sends = [lambda n, hop=hop: send_to(n, *hop) for hop in hops[1:]]
    targets = jnp.asarray([[local * send_to(n, *hop) for hop in hops] for n in everyone], jnp.int32)
    first_expert = targets[lax.axis_index("expert")]

    joined, own = call(
        head_kernel,
        "head",
        [
            jax.ShapeDtypeStruct((local, slice_rows + 64, lift_width), BF),
            jax.ShapeDtypeStruct((2 * tok + 16, width), BF),
        ],
        in_specs=[vm] * 6,
        out_specs=[vm] * 2,
        nbytes=2 << 20,
        vmem=56,
    )(expert_ids.T, combine_weights.T, tokens, cotangent, lift_weights, down_weights)
    weights = lax.all_gather(joined, "dp")

    bundles = [own] + [permute(own, target) for target in shared]
    chunk_shape = jax.ShapeDtypeStruct((2, local, SIDE * CAP, width), BF)
    pack_flops = 2 * experts * CAP * tok * width
    table_scratch = pltpu.VMEM((SIDE, experts + SPARE, tok), F32)
    packed = call(
        pack_kernel,
        "pack",
        [pltpu.VMEM(chunk_shape.shape, BF)] * count,
        in_specs=[smem] + [vm] * SIDE,
        out_specs=[vm] * count,
        scratch=[table_scratch, table_scratch],
        flops=2 * pack_flops,
        vmem=32,
        nbytes=16 << 20,
    )(first_expert, offchip(own), *[onchip(x) for x in bundles[1:]])
    chunks = list(packed[:1]) + [permute(x, target) for x, target in zip(packed[1:], sends)]
    slot_rows = local * count * CAP
    picks = call(
        functools.partial(plan_kernel, count),
        "plan",
        jax.ShapeDtypeStruct((2, SIDE, 2 * tok, slot_rows), BF),
        grid=(1,),
        in_specs=[smem]
        + [pl.BlockSpec((16, width), lambda i: (2 * tok // 16, 0))] * SIDE
        + [pl.BlockSpec(memory_space=pl.ANY)],
        out_specs=pl.BlockSpec((2, SIDE, 2 * tok, slot_rows), lambda i: (0, 0, 0, 0)),
        scratch=[table_scratch, table_scratch],
        nbytes=2 << 20,
    )(first_expert, *bundles, packed[0])

    weight_block = pl.BlockSpec((groups, 1, slice_rows + 64, lift_width), lambda e: (0, e, 0, 0))
    back_shape = jax.ShapeDtypeStruct((2, SIDE, local, CAP, width), BF)
    back_block = pl.BlockSpec((2, SIDE, 1, CAP, width), lambda e: (0, 0, e, 0, 0))
    unit = 2 * local * filled * ff * width
    *returns, weight_grads = call(
        functools.partial(expert_kernel, count),
        "expert",
        [back_shape] * count
        + [jax.ShapeDtypeStruct((groups, local, slice_rows + 64, lift_width), BF)],
        grid=(local,),
        in_specs=[pl.BlockSpec((2, 1, SIDE * CAP, width), lambda e: (0, e, 0, 0))] * count
        + [weight_block, pl.BlockSpec(memory_space=pl.ANY)],
        out_specs=[back_block] * count + [weight_block],
        flops=9 * unit,
        vmem=56,
        nbytes=24 << 20,
    )(*[offchip(x) for x in chunks], weights, picks)
    summed = lax.psum_scatter(weight_grads, "dp", scatter_dimension=0, tiled=False)
    returns = [x.reshape(2, SIDE, local * CAP, width) for x in returns]
    order = [0] + sorted(range(1, count), key=lambda p: (-hops[p][0] % SIDE, hops[p][1]))
    parts = [restore(returns[p], sends[p - 1]) if p else returns[0] for p in order]
    combining = functools.partial(combine_kernel, [order.index(p) for p in range(count)])
    sum_block = pl.BlockSpec((1, tok, width), lambda i: (i, 0, 0))
    sums = call(
        combining,
        "combine",
        [jax.ShapeDtypeStruct((2, tok, width), F32)] + [jax.ShapeDtypeStruct((2, tok, width), BF)] * (SIDE - 1),
        grid=(2,),
        in_specs=[pl.BlockSpec((1, SIDE, 2 * tok, slot_rows), lambda i: (i, 0, 0, 0))]
        + [pl.BlockSpec((1, SIDE, local * CAP, width), lambda i: (i, 0, 0, 0))] * count,
        out_specs=[sum_block] * SIDE,
        flops=4 * pack_flops,
        nbytes=10 << 20,
    )(picks, *parts)
    sums = list(sums[:1]) + [restore(x, target) for x, target in zip(sums[1:], shared)]
    token_shape = jax.ShapeDtypeStruct((tok, width), BF)
    layer_output, token_grads = call(
        total_kernel,
        "total",
        [token_shape, token_shape],
        in_specs=[vm] * SIDE,
        out_specs=[vm] * 2,
        nbytes=3 << 20,
    )(*sums)
    lift_grads, down_grads = call(
        split_kernel,
        "split",
        [jax.ShapeDtypeStruct(lift_weights.shape, BF), jax.ShapeDtypeStruct(down_weights.shape, BF)],
        in_specs=[vm],
        out_specs=[vm] * 2,
        nbytes=1 << 20,
    )(offchip(summed))
    return (layer_output, token_grads, lift_grads, down_grads)


def solution(mesh):
    rows = P(("expert", "dp"), None)
    lift, down = P("expert", "dp", None), P("expert", None, "dp")
    return jax.shard_map(
        shards,
        mesh=mesh,
        in_specs=(rows, rows, rows, lift, down, rows),
        out_specs=(rows, rows, lift, down),
        check_vma=False,
    )
```
